256 devices in a mesh: row: 8 (over z), col: 32 (over x, y, core).
Axes of the slice: x: 4, y: 4, z: 8, core: 2. Of those that a mesh axis runs over, the one named last changes fastest.
Arguments:
- covariance: float32 [4, 8, 512, 2, 32, 256], P(None, 'row', None, None, 'col'), may hold values from 0 to 24, as said below
- noise: float32 [1024, 2048], P(None, 'col'), may hold values from -6 to 6
Outputs:
- factored: float32 [4, 8, 512, 2, 32, 256], P(None, 'row', None, None, 'col')
- realize: float32 [4, 8, 512, 2048], P(None, 'row', None, 'col')
The draws below stay inside these ranges and needn't reach their ends.
Inputs may be any that keep to these rules, and one draw needn't show every extreme that they name: covariance is symmetric and positive definite.
All inputs are finite; a program needn't handle non-finite values.
Results may differ from the reference program's by a relative error of at most 0.0003.
Values sent between devices are 32-bit elements; how exact they have to be, the bound alone decides.
No kernel may reach another device: no remote copies, remote signals or barrier semaphores. Data moves between devices by JAX's collectives and lax.ppermute only.
A program may use at most 128 MiB of HBM per device.

```python
import math
import jax
import jax.numpy as jnp
from jax import lax

ORDER = 16384
TILE = 512
HALF = 256
PANELS = 2
REAL = 2048
ROW_CYCLES = 4
COL_CYCLES = 2
N_ROW = 8
N_COL = 32


long_range = 600.0


long_sill = 0.8


short_range = 24.0


short_sill = 0.2


nugget = 0.5


east_cells = 2048


north_cells = 512


def matern_three_halves(distance, kernel_range):
    scaled = distance * (math.sqrt(3.0) / kernel_range)
    return (1.0 + scaled) * jnp.exp(-scaled)


def draw_covariance(key, part):
    east = jax.random.randint(jax.random.fold_in(key, 11), (ORDER,), 0, east_cells)
    north = jax.random.randint(jax.random.fold_in(key, 12), (ORDER,), 0, north_cells)
    all_ids = jnp.arange(ORDER, dtype=jnp.int32)
    scales = jnp.exp(0.1 * jax.random.uniform(jax.random.fold_in(key, 14), (ORDER,), jnp.float32))

    def row_block(block_index):
        first_row = block_index * TILE
        east_rows = lax.dynamic_slice_in_dim(east, first_row, TILE)
        north_rows = lax.dynamic_slice_in_dim(north, first_row, TILE)
        scale_rows = lax.dynamic_slice_in_dim(scales, first_row, TILE)
        row_ids = first_row + jnp.arange(TILE, dtype=jnp.int32)
        delta_east = east_rows[:, None] - east[None, :]
        delta_north = north_rows[:, None] - north[None, :]
        squared = delta_east * delta_east + delta_north * delta_north
        distance = jnp.sqrt(squared.astype(jnp.float32))
        values = long_sill * matern_three_halves(distance, long_range)
        values = values + short_sill * matern_three_halves(distance, short_range)
        values = values + nugget * (row_ids[:, None] == all_ids[None, :]).astype(jnp.float32)
        return values * scale_rows[:, None] * scales[None, :]
    full = lax.map(row_block, jnp.arange(ORDER // TILE, dtype=jnp.int32))
    full = full.reshape(ROW_CYCLES, N_ROW, TILE, COL_CYCLES, N_COL, HALF)
    return jnp.flip(full, axis=4)


def shard_levels(key, dims, split, low, top_value):
    loudness, own = 1.0, jax.random.fold_in(key, 6)
    for position, shards_of in split:
        draws = jnp.exp(jax.random.uniform(jax.random.fold_in(own, position), (shards_of,), jnp.float32, low / len(split), top_value / len(split)))
        loudness = loudness * jnp.repeat(draws, dims[position] // shards_of).reshape([-1 if axis == position else 1 for axis in range(len(dims))])
    return loudness


def scatter_about(rng, dims, width, limit, split=(), held_as=jnp.bfloat16):
    level = shard_levels(rng, dims, split, -0.22, 0.18) if split else 1.0
    array = jax.random.normal(rng, dims, jnp.float32) * width * level
    return jnp.minimum(jnp.maximum(array, -limit), limit).astype(held_as)


def setup_inputs(seed: int = 0) -> dict:
    splits = jax.random.split(jax.random.key(seed), 3)
    covariance = draw_covariance(jax.random.fold_in(splits[2], 71), 0)
    noise = scatter_about(splits[1], (PANELS * TILE, REAL), 1.0, 6.0, ((1, 32),), jnp.float32)
    return dict(covariance=covariance, noise=noise)


def panel_factor(column_block, offset):
    factor = jnp.linalg.cholesky(column_block[offset:offset + TILE])
    solved = lax.linalg.triangular_solve(factor, column_block, left_side=False, lower=True, transpose_a=True)
    all_ids = jnp.arange(ORDER, dtype=jnp.int32)
    result = jnp.where(all_ids[:, None] < offset, jnp.zeros_like(solved), solved)
    return result.at[offset:offset + TILE].set(factor)

def reference(covariance, noise):
    highest = lax.Precision.HIGHEST
    matrix = jnp.flip(covariance, axis=4).reshape(ORDER, ORDER)
    panels = []
    for panel in range(PANELS):
        offset = panel * TILE
        column_block = matrix[:, offset:offset + TILE]
        if panel > 0:
            earlier = jnp.concatenate(panels, axis=1)
            column_block = column_block - jnp.dot(earlier, earlier[offset:offset + TILE].T, precision=highest)
        panels.append(panel_factor(column_block, offset))
    panel_cols = jnp.concatenate(panels, axis=1)
    realize = jnp.dot(panel_cols, noise, precision=highest)
    panel_width = PANELS * TILE
    all_ids = jnp.arange(ORDER, dtype=jnp.int32)

    def row_block(block_index):
        first_row = block_index * TILE
        rows_now = lax.dynamic_slice_in_dim(matrix, first_row, TILE, 0)
        left_part = lax.dynamic_slice_in_dim(panel_cols, first_row, TILE, 0)
        trailing = rows_now - jnp.dot(left_part, panel_cols.T, precision=highest)
        merged = jnp.concatenate([left_part, trailing[:, panel_width:]], axis=1)
        row_ids = first_row + jnp.arange(TILE, dtype=jnp.int32)
        return jnp.where(row_ids[:, None] >= all_ids[None, :], merged, jnp.zeros_like(merged))
    factored = lax.map(row_block, jnp.arange(ORDER // TILE, dtype=jnp.int32))
    factored = factored.reshape(ROW_CYCLES, N_ROW, TILE, COL_CYCLES, N_COL, HALF)
    factored = jnp.flip(factored, axis=4)
    return (factored, realize.reshape(ROW_CYCLES, N_ROW, TILE, REAL))
```

```python
import functools

import jax
import jax.numpy as jnp
from jax import lax
from jax.experimental import pallas as pl
from jax.experimental.pallas import tpu as pltpu
from jax.sharding import PartitionSpec as P


TILE = 512
HALF = 256
WIDTH = 1024
BLK = 128
SUB = 8
ZS, XS, YS = 8, 4, 4
AXES = ("row", "col")
HI = lax.Precision.HIGHEST
F32 = jnp.float32


def device_at(z, x, y, k):
    return (z % ZS) * 32 + 31 - ((((x % XS) * YS) + (y % YS)) * 2 + k)


def moved(value, pairs):
    return lax.ppermute(value, AXES, [(device_at(*a), device_at(*b)) for a, b in pairs])


def shifted(value, dz=0, dx=0, dy=0, swap=0):
    return moved(
        value,
        [
            ((z, x, y, k), (z + dz, x + dx, y + dy, k ^ swap))
            for z in range(ZS)
            for x in range(XS)
            for y in range(YS)
            for k in range(2)
        ],
    )


def turned(parts, first):
    count = len(parts)
    out = []
    for j in range(count):
        at = jnp.mod(first - j, count)
        value = parts[0]
        for i in range(1, count):
            value = jnp.where(at == i, parts[i], value)
        out.append(value)
    return jnp.stack(out)


def after(trigger, *values):
    return lax.optimization_barrier((trigger, *values))[1:]


def tied(*values):
    return lax.optimization_barrier(values)


def dot_nt(a, b):
    return lax.dot_general(a, b, (((1,), (1,)), ((), ())), precision=HI, preferred_element_type=F32)


def dot_nn(a, b):
    return lax.dot_general(a, b, (((1,), (0,)), ((), ())), precision=HI, preferred_element_type=F32)


def dot_tn(a, b):
    return lax.dot_general(a, b, (((0,), (0,)), ((), ())), precision=HI, preferred_element_type=F32)


def halves(value):
    high = value.astype(jnp.bfloat16)
    return high, (value - high.astype(F32)).astype(jnp.bfloat16)


def product(a, b, contract):
    (ah, al), (bh, bl) = a, b
    dims = (contract, ((), ()))
    parts = [
        lax.dot_general(u, v, dims, preferred_element_type=F32) for u, v in ((ah, bl), (al, bh), (ah, bh))
    ]
    return parts[0] + parts[1] + parts[2]


NN = ((1,), (0,))


def eliminate(block):
    count = BLK // SUB
    s = [block[SUB * t : SUB * (t + 1), :] for t in range(count)]
    lane = lax.broadcasted_iota(jnp.int32, (SUB, BLK), 1)
    sub = lax.broadcasted_iota(jnp.int32, (SUB, BLK), 0)
    e = [(lane == sub + SUB * t).astype(F32) for t in range(count)]

    def row_of(x, i):
        return jnp.broadcast_to(x[i : i + 1, :], (SUB, BLK))

    def col_of(x, j):
        return jnp.broadcast_to(x[:, j : j + 1], (SUB, BLK))

    upper, inverse = [], []
    for t in range(count):
        c = [col_of(s[t], SUB * t + j) for j in range(SUB)]
        r, x = s[t], e[t]
        ur = jnp.zeros((SUB, BLK), F32)
        ux, dd, iv = ur, ur, ur
        for i in range(SUB):
            p = row_of(c[i], i)
            inv = 1.0 / p
            rr, rx = row_of(r, i), row_of(x, i)
            here = sub == i
            ur = jnp.where(here, rr, ur)
            ux = jnp.where(here, rx, ux)
            dd = jnp.where(here, p, dd)
            iv = jnp.where(here, inv, iv)
            mult = jnp.where(here, 0.0, c[i] * inv)
            for j in range(i + 1, SUB):
                c[j] = c[j] - mult * row_of(c[j], i)
            r = r - mult * rr
            x = x - mult * rx
        scale = lax.rsqrt(dd)
        upper.append(ur * scale)
        inverse.append(ux * scale)
        if t + 1 < count:
            w, v = r * iv, x * iv
            wb = [row_of(w, j) for j in range(SUB)]
            vb = [row_of(v, j) for j in range(SUB)]
            for u in range(t + 1, count):
                su, eu = s[u], e[u]
                for j in range(SUB):
                    cu = col_of(s[u], SUB * t + j)
                    su = su - cu * wb[j]
                    eu = eu - cu * vb[j]
                s[u], e[u] = su, eu
    upper = jnp.concatenate(upper, axis=0)
    inverse = jnp.concatenate(inverse, axis=0)
    rows = lax.broadcasted_iota(jnp.int32, (BLK, BLK), 0)
    lanes = lax.broadcasted_iota(jnp.int32, (BLK, BLK), 1)
    return jnp.where(rows <= lanes, upper, 0.0), jnp.where(rows >= lanes, inverse, 0.0)


def factor_kernel(first, count, fresh, *refs):
    if fresh:
        a_ref, s_ref, x_ref = refs
        n = a_ref.shape[0]
        rows = lax.broadcasted_iota(jnp.int32, (n, n), 0)
        lanes = lax.broadcasted_iota(jnp.int32, (n, n), 1)
        x_ref[...] = (rows == lanes).astype(F32)
    else:
        a_ref, xin_ref, s_ref, x_ref = refs
        n = a_ref.shape[0]
        x_ref[...] = xin_ref[...]
    s_ref[...] = a_ref[...]
    below = lax.broadcasted_iota(jnp.int32, (n, BLK), 0)

    def step(k, carry):
        at = pl.multiple_of(k * BLK, BLK)
        here = pl.ds(at, BLK)
        _, inv = eliminate(s_ref[here, here])
        pan = jnp.where(below >= at + BLK, dot_nt(s_ref[:, here], inv), 0.0)
        s_ref[...] = s_ref[...] - dot_nt(pan, pan)
        ek = dot_nn(inv, x_ref[here, :])
        x_ref[...] = x_ref[...] - dot_nn(pan, ek)
        x_ref[here, :] = ek
        return carry

    lax.fori_loop(first, first + count, step, 0)


def factor_stage(first, count, *state):
    n = state[0].shape[0]
    shape = jax.ShapeDtypeStruct((n, n), F32)
    return pl.pallas_call(
        functools.partial(factor_kernel, first, count, len(state) == 1),
        out_shape=(shape, shape),
        in_specs=[pl.BlockSpec(memory_space=pltpu.VMEM)] * len(state),
        out_specs=(pl.BlockSpec(memory_space=pltpu.VMEM),) * 2,
        cost_estimate=pl.CostEstimate(flops=2 * 10**10, bytes_accessed=4 * n * n * 4, transcendentals=0),
        name="factor_stage",
    )(*state)


def unpack_kernel(v_ref, own_ref, cross_ref):
    for q in range(2):
        own_ref[0, :, q * BLK : (q + 1) * BLK] = v_ref[pl.ds(q, TILE, stride=4), :]

    @pl.when(pl.program_id(0) == 0)
    def _():
        for q in range(4):
            cross_ref[:, q * BLK : (q + 1) * BLK] = v_ref[pl.ds(q, TILE, stride=4), :]


def unpack(view):
    return pl.pallas_call(
        unpack_kernel,
        out_shape=(
            jax.ShapeDtypeStruct((4, TILE, HALF), F32),
            jax.ShapeDtypeStruct((TILE, 2 * HALF), F32),
        ),
        grid=(4,),
        in_specs=[pl.BlockSpec((4 * TILE, BLK), lambda a: (a, 0))],
        out_specs=(
            pl.BlockSpec((1, TILE, HALF), lambda a: (a, 0, 0)),
            pl.BlockSpec((TILE, 2 * HALF), lambda a: (0, 0)),
        ),
        name="unpack",
    )(view)


ROWS = 256


def apply_kernel(meta, v_ref, high_ref, low_ref, noise_ref, *refs):
    held, (out_ref, real_ref, buf, sem) = refs[:8], refs[8:]
    step = pl.program_id(0)
    tile, plane, pos, core, owner = meta[step], meta[4], meta[5], meta[6], meta[7]

    def copies(i):
        return [
            pltpu.make_async_copy(held[2 * i + m], buf.at[i % 2, m], sem.at[i % 2, m]) for m in range(2)
        ]

    @pl.when(step == 0)
    def _():
        for copy in copies(0):
            copy.start()

    for i in range(4):

        @pl.when(step == i)
        def _():
            if i < 3:
                for copy in copies(i + 1):
                    copy.start()
            for copy in copies(i):
                copy.wait()

    slot = step % 2

    def part(at, carry):
        first = pl.multiple_of(at * ROWS, ROWS)
        rows = pl.ds(first, ROWS)
        acc = real = None
        for m in range(2):
            for panel in range(2):
                block = 2 * panel + (core if m == 0 else 1 - core)
                here = pl.ds(pl.multiple_of(block * HALF, HALF), HALF)
                value = buf[slot, m, panel, rows, :]
                term = product(halves(value), (high_ref[here, :], low_ref[here, :]), NN)
                drawn = dot_nn(value, noise_ref[here, :])
                acc = term if acc is None else acc + term
                real = drawn if real is None else real + drawn
        row = (tile * ZS + plane) * TILE + first + lax.broadcasted_iota(jnp.int32, (ROWS, BLK), 0)
        lane = lax.broadcasted_iota(jnp.int32, (ROWS, BLK), 1)
        for q in range(4):
            there = pl.ds(4 * first + q, ROWS, stride=4)
            base = v_ref[there, :]
            if q < 2:
                base = jnp.where(owner == 1, 0.0, base)
            col = ((q // 2) * 32 + pos) * HALF + (q % 2) * BLK + lane
            res = base - acc[:, q * BLK : (q + 1) * BLK]
            out_ref[there, :] = jnp.where(row >= col, res, 0.0)
        real_ref[0, :, rows] = real.T
        return carry

    lax.fori_loop(0, TILE // ROWS, part, 0)


def apply_all(meta, view, high, low, drawn, held):
    wide = pl.BlockSpec((4 * TILE, BLK), lambda i, m: (m[i], 0))
    real = drawn.shape[1]

    def whole(shape):
        return pl.BlockSpec(shape, lambda i, m: (0, 0))

    return pl.pallas_call(
        apply_kernel,
        out_shape=(
            jax.ShapeDtypeStruct(view.shape, F32),
            jax.ShapeDtypeStruct((4, real, TILE), F32),
        ),
        grid_spec=pltpu.PrefetchScalarGridSpec(
            num_scalar_prefetch=1,
            grid=(4,),
            in_specs=[wide, whole(high.shape), whole(low.shape), whole(drawn.shape)]
            + [pl.BlockSpec(memory_space=pl.ANY)] * len(held),
            out_specs=(wide, pl.BlockSpec((1, real, TILE), lambda i, m: (m[i], 0, 0))),
            scratch_shapes=[
                pltpu.VMEM((2, 2, 2, TILE, HALF), F32),
                pltpu.SemaphoreType.DMA((2, 2)),
            ],
        ),
        cost_estimate=pl.CostEstimate(flops=2 * 10**10, bytes_accessed=24 * 2**20, transcendentals=0),
        name="apply_all",
    )(meta, view, high, low, drawn, *held)


def weights_kernel(meta, x11, x22, l21, y1, rest, noise, high_ref, low_ref, drawn_ref):
    pos, owner = meta[5], meta[7]
    y2 = dot_nn(x22[...], rest[...])

    def rhs(part, at):
        ids = at + lax.broadcasted_iota(jnp.int32, (TILE, HALF), 0)
        spot = pos * HALF + lax.broadcasted_iota(jnp.int32, (TILE, HALF), 1)
        first = jnp.where(owner == 1, jnp.where(ids == spot, -1.0, 0.0), part[:, :HALF])
        return jnp.concatenate([first, part[:, HALF:], noise[at : at + TILE, :]], axis=1)

    w2 = dot_tn(x22[...], rhs(y2, TILE))
    w1 = dot_tn(x11[...], rhs(y1[...], 0) - dot_tn(l21[...], w2))
    for at, value in ((0, w1), (TILE, w2)):
        here = pl.ds(at, TILE)
        high_ref[here, :], low_ref[here, :] = halves(value[:, :TILE])
        drawn_ref[here, :] = value[:, TILE:]


def make_weights(meta, x11, x22, l21, y1, rest, noise):
    split = jax.ShapeDtypeStruct((WIDTH, TILE), jnp.bfloat16)
    vmem = pl.BlockSpec(memory_space=pltpu.VMEM)
    return pl.pallas_call(
        weights_kernel,
        out_shape=(split, split, jax.ShapeDtypeStruct(noise.shape, F32)),
        in_specs=[pl.BlockSpec(memory_space=pltpu.SMEM)] + [vmem] * 6,
        out_specs=(vmem,) * 3,
        cost_estimate=pl.CostEstimate(flops=15 * 10**9, bytes_accessed=8 * 2**20, transcendentals=0),
        name="make_weights",
    )(meta, x11, x22, l21, y1, rest, noise)


def scattered_along_x(parts):
    got = []
    for d in (1, 2, 3):
        pairs = [((pz, 0, py, c), (pz, d, py, c)) for pz in range(ZS) for py in (0, 1) for c in range(2)]
        got.append(moved(parts[d], pairs))
    return got[0] + got[1] + got[2]


def planes(routes, value):
    return moved(
        value,
        [
            ((a, px, py, c), (b, px, py, c))
            for a, b in routes
            for px in range(XS)
            for py in range(YS)
            for c in range(2)
        ],
    )


def doubled_one(hold, z):
    got = planes(((0, 6), (1, 3)), hold)
    return jnp.where((z == 6) | (z == 3), got, hold)


def doubled_two(hold, z):
    got = planes(((0, 2), (6, 4), (1, 7), (3, 5)), hold)
    return jnp.where((z == 2) | (z == 4) | (z == 7) | (z == 5), got, hold)


def exchanged(hold, z):
    got = planes([(a, a ^ 1) for a in range(ZS)], hold)
    even = z % 2 == 0
    return jnp.where(even, hold, got), jnp.where(even, got, hold)


def square_quarter(tile, x):
    return jnp.where(x == 0, tile[:128], scattered_along_x([tile[128 * d : 128 * (d + 1)] for d in range(4)]))


def square_chunks(got, y):
    arrived = [got[:32]]
    for d in (1, 2, 3):
        pairs = [
            ((pz, px, py, c), (pz, px, py + d, c)) for pz in (0, 1) for px in range(XS) for py in (0, 1) for c in range(2)
        ]
        arrived.append(moved(got[32 * d : 32 * (d + 1)], pairs))

    def picked(at):
        return jnp.where(at == 0, arrived[0], jnp.where(at == 1, arrived[1], jnp.where(at == 2, arrived[2], arrived[3])))

    return jnp.stack([picked(y), picked(jnp.mod(y - 1, YS))])


def gathered_along_y(parts, firsts, y):
    ring = [parts] + [shifted(parts, dy=d) for d in (1, 2, 3)]
    return jnp.stack(
        [turned([p[m] for p in ring], jnp.mod(y - f, YS)).reshape(128, HALF) for m, f in enumerate(firsts)]
    )


def gathered_along_x(line, x):
    ring = [line] + [shifted(line, dx=d) for d in (1, 2, 3)]
    return jnp.moveaxis(turned(ring, x), 0, 1).reshape(line.shape[0], TILE, HALF)


def both_cores(mine, k):
    other = shifted(mine, swap=1)
    return jnp.where(
        k == 0, jnp.concatenate([mine, other], axis=2), jnp.concatenate([other, mine], axis=2)
    )


def y_hop(routes, value):
    return moved(
        value,
        [((pz, px, a, c), (pz, px, b, c)) for a, b in routes for pz in range(ZS) for px in range(XS) for c in range(2)],
    )


def shards(covariance, noise):
    z = lax.axis_index("row").astype(jnp.int32)
    pos = 31 - lax.axis_index("col").astype(jnp.int32)
    x, y, k = pos // 8, (pos // 2) % 4, pos % 2
    owner = (pos < 4).astype(jnp.int32)
    view = covariance.reshape(-1, BLK)
    own, cross = unpack(view)

    meta = jnp.stack([x, jnp.mod(x + 3, XS), jnp.mod(x + 1, XS), jnp.mod(x + 2, XS), z, pos, k, owner])
    quarter = square_quarter(own[0], x)
    own = after(quarter, own)[0]
    hold = square_chunks(quarter, y)
    tile = jnp.where(x == 0, own[0], scattered_along_x(own))
    hold = doubled_one(hold, z)
    hold = doubled_two(hold, z)
    first, later = exchanged(hold, z)
    cross = after(first, cross)[0]
    cross = doubled_one(cross, z)
    line = gathered_along_y(first[:1], (0,), y)
    tile, later = after(line, tile, later)
    near = y_hop(((0, 1), (1, 0)), tile)
    mine = gathered_along_x(line, x)
    late_line = gathered_along_y(later, (0, 1), y)
    a11 = both_cores(mine, k)[0]
    a11, late_line, near = tied(a11, late_line, near)
    pair = jnp.stack([jnp.where(y == 0, tile, near), jnp.where(y == 0, near, tile)])
    spread = y_hop(((0, 3), (1, 2)), pair)
    state = factor_stage(0, 2, a11)
    late = gathered_along_x(late_line, x)
    s1, s2, late, cross = tied(*state, late, cross)
    cross = doubled_two(cross, z)
    late = both_cores(late, k)
    _, x11 = factor_stage(2, 2, s1, s2)
    x11, spread, late, cross = tied(x11, spread, late, cross)
    pieces = jnp.where(y < 2, pair, spread)
    a21, a22 = late[0], late[1]
    up, down = shifted(pieces, dx=1), shifted(pieces, dx=-1)
    c0, c1 = exchanged(cross, z)
    l21 = dot_nt(a21, x11)
    state = factor_stage(0, 2, a22 - dot_nt(l21, l21))
    s1, s2, up, down, c0, c1 = tied(*state, up, down, c0, c1)
    far = shifted(up, dx=1)
    swaps = [shifted(held, swap=1) for held in (pieces, up, down)]
    y1 = dot_nn(x11, c0)
    rest = c1 - dot_nn(l21, y1)
    _, x22 = factor_stage(2, 2, s1, s2)
    x22, far = tied(x22, far)
    swaps.append(shifted(far, swap=1))
    high, low, drawn = make_weights(meta, x11, x22, l21, y1, rest, noise)
    held = [piece for pair in zip((pieces, up, down, far), swaps) for piece in pair]
    factored, real = apply_all(meta, view, high, low, drawn, held)
    return factored.reshape(covariance.shape), jnp.swapaxes(real, 1, 2)[:, None]


def solution(mesh):
    placed = (P(None, "row", None, None, "col", None), P(None, "col"))
    return jax.shard_map(
        shards,
        mesh=mesh,
        in_specs=placed,
        out_specs=(P(None, "row", None, None, "col", None), P(None, "row", None, "col")),
        check_vma=False,
    )
```

```python
import jax
import jax.numpy as jnp
from jax import lax
from jax.experimental import pallas as pl
from jax.experimental.pallas import tpu as pltpu
from jax.sharding import PartitionSpec as P


TILE = 512
HALF = 256
WIDTH = 1024
BLK = 128
SUB = 8
ZS, XS, YS = 8, 4, 4
AXES = ("row", "col")
HI = lax.Precision.HIGHEST
F32 = jnp.float32


def device_at(z, x, y, k):
    return (z % ZS) * 32 + 31 - ((((x % XS) * YS) + (y % YS)) * 2 + k)


def moved(value, pairs):
    return lax.ppermute(value, AXES, [(device_at(*a), device_at(*b)) for a, b in pairs])


def shifted(value, dz=0, dx=0, dy=0, swap=0):
    return moved(
        value,
        [
            ((z, x, y, k), (z + dz, x + dx, y + dy, k ^ swap))
            for z in range(ZS)
            for x in range(XS)
            for y in range(YS)
            for k in range(2)
        ],
    )


def turned(parts, first):
    count = len(parts)
    out = []
    for j in range(count):
        at = jnp.mod(first - j, count)
        value = parts[0]
        for i in range(1, count):
            value = jnp.where(at == i, parts[i], value)
        out.append(value)
    return jnp.stack(out)


def after(trigger, *values):
    return lax.optimization_barrier((trigger, *values))[1:]


def tied(*values):
    return lax.optimization_barrier(values)


def dot_nt(a, b):
    return lax.dot_general(a, b, (((1,), (1,)), ((), ())), precision=HI, preferred_element_type=F32)


def dot_nn(a, b):
    return lax.dot_general(a, b, (((1,), (0,)), ((), ())), precision=HI, preferred_element_type=F32)


def dot_tn(a, b):
    return lax.dot_general(a, b, (((0,), (0,)), ((), ())), precision=HI, preferred_element_type=F32)


def halves(value):
    high = value.astype(jnp.bfloat16)
    return high, (value - high.astype(F32)).astype(jnp.bfloat16)


def thirds(value):
    first, rest = value.astype(jnp.bfloat16), value
    rest = rest - first.astype(F32)
    second = rest.astype(jnp.bfloat16)
    return first, second, (rest - second.astype(F32)).astype(jnp.bfloat16)


NN = ((1,), (0,))


def eliminate(block):
    count = BLK // SUB
    s = [block[SUB * t : SUB * (t + 1), :] for t in range(count)]
    lane = lax.broadcasted_iota(jnp.int32, (SUB, BLK), 1)
    sub = lax.broadcasted_iota(jnp.int32, (SUB, BLK), 0)
    e = [(lane == sub + SUB * t).astype(F32) for t in range(count)]

    def row_of(x, i):
        return jnp.broadcast_to(x[i : i + 1, :], (SUB, BLK))

    def col_of(x, j):
        return jnp.broadcast_to(x[:, j : j + 1], (SUB, BLK))

    inverse = []
    for t in range(count):
        c = [col_of(s[t], SUB * t + j) for j in range(SUB)]
        r, x = s[t], e[t]
        ux = jnp.zeros((SUB, BLK), F32)
        dd, iv = ux, ux
        for i in range(SUB):
            p = row_of(c[i], i)
            inv = 1.0 / p
            rr, rx = row_of(r, i), row_of(x, i)
            here = sub == i
            ux = jnp.where(here, rx, ux)
            dd = jnp.where(here, p, dd)
            iv = jnp.where(here, inv, iv)
            mult = jnp.where(here, 0.0, c[i] * inv)
            for j in range(i + 1, SUB):
                c[j] = c[j] - mult * row_of(c[j], i)
            r = r - mult * rr
            x = x - mult * rx
        inverse.append(ux * lax.rsqrt(dd))
        if t + 1 < count:
            w, v = r * iv, x * iv
            wb = [row_of(w, j) for j in range(SUB)]
            vb = [row_of(v, j) for j in range(SUB)]
            for u in range(t + 1, count):
                su, eu = s[u], e[u]
                for j in range(SUB):
                    cu = col_of(s[u], SUB * t + j)
                    su = su - cu * wb[j]
                    eu = eu - cu * vb[j]
                s[u], e[u] = su, eu
    inverse = jnp.concatenate(inverse, axis=0)
    rows = lax.broadcasted_iota(jnp.int32, (BLK, BLK), 0)
    lanes = lax.broadcasted_iota(jnp.int32, (BLK, BLK), 1)
    return jnp.where(rows >= lanes, inverse, 0.0)


def eliminate_blocks(first, count, s_ref, x_ref, p_ref):
    n = s_ref.shape[0]
    blocks = n // BLK
    below = lax.broadcasted_iota(jnp.int32, (n, BLK), 0)

    def step(k, carry):
        at = pl.multiple_of(k * BLK, BLK)
        here = pl.ds(at, BLK)
        inv = eliminate(s_ref[here, here])
        p_ref[...] = jnp.where(below >= at + BLK, dot_nt(s_ref[:, here], inv), 0.0)
        ek = dot_nn(inv, x_ref[here, :])
        x_ref[here, :] = ek

        def under(i, inner):
            rows = pl.ds(pl.multiple_of(i * BLK, BLK), BLK)
            part = p_ref[rows, :]
            s_ref[rows, :] = s_ref[rows, :] - dot_nt(part, p_ref[...])
            x_ref[rows, :] = x_ref[rows, :] - dot_nn(part, ek)
            return inner

        lax.fori_loop(k + 1, blocks, under, 0)
        return carry

    lax.fori_loop(first, first + count, step, 0)


def set_identity(x_ref):
    rows = lax.broadcasted_iota(jnp.int32, x_ref.shape, 0)
    lanes = lax.broadcasted_iota(jnp.int32, x_ref.shape, 1)
    x_ref[...] = (rows == lanes).astype(F32)


def joined(core, s_ref, mine, other):
    @pl.when(core == 0)
    def _():
        s_ref[:, :HALF] = mine
        s_ref[:, HALF:] = other

    @pl.when(core == 1)
    def _():
        s_ref[:, :HALF] = other
        s_ref[:, HALF:] = mine


def first_kernel(meta, mine_ref, other_ref, s_ref, x_ref, p_ref):
    joined(meta[6], s_ref, mine_ref[...], other_ref[...])
    set_identity(x_ref)
    eliminate_blocks(0, 2, s_ref, x_ref, p_ref)


def second_kernel(meta, mine_ref, other_ref, x11_ref, s_ref, x_ref, l21_ref, p_ref):
    joined(meta[6], s_ref, mine_ref[0], other_ref[0])
    l21_ref[...] = dot_nt(s_ref[...], x11_ref[...])
    joined(meta[6], s_ref, mine_ref[1], other_ref[1])

    def rows(i, carry):
        here = pl.ds(pl.multiple_of(i * BLK, BLK), BLK)
        s_ref[here, :] = s_ref[here, :] - dot_nt(l21_ref[here, :], l21_ref[...])
        return carry

    lax.fori_loop(0, TILE // BLK, rows, 0)
    set_identity(x_ref)
    eliminate_blocks(0, 2, s_ref, x_ref, p_ref)


def last_kernel(sin_ref, xin_ref, x_ref, s_ref, p_ref):
    s_ref[...] = sin_ref[...]
    x_ref[...] = xin_ref[...]
    eliminate_blocks(2, 2, s_ref, x_ref, p_ref)


def stage(kernel, args, outs, scratch, with_meta):
    vmem = pl.BlockSpec(memory_space=pltpu.VMEM)
    specs = [pl.BlockSpec(memory_space=pltpu.SMEM)] if with_meta else []
    square = jax.ShapeDtypeStruct((TILE, TILE), F32)
    return pl.pallas_call(
        kernel,
        out_shape=(square,) * outs,
        in_specs=specs + [vmem] * (len(args) - len(specs)),
        out_specs=(vmem,) * outs,
        scratch_shapes=scratch + [pltpu.VMEM((TILE, BLK), F32)],
        cost_estimate=pl.CostEstimate(flops=2 * 10**10, bytes_accessed=4 * 2**20, transcendentals=0),
    )(*args)


def first_half(meta, mine, other):
    return stage(first_kernel, (meta, mine, other), 2, [], True)


def second_half(meta, mine, other, x11):
    return stage(second_kernel, (meta, mine, other, x11), 3, [], True)


def rest_of(s, x):
    return stage(last_kernel, (s, x), 1, [pltpu.VMEM((TILE, TILE), F32)], False)[0]


def unpack_first_kernel(v_ref, tile_ref, cross_ref, *quarters):
    for q in range(4):
        piece = v_ref[pl.ds(q, TILE, stride=4), :]
        cross_ref[:, q * BLK : (q + 1) * BLK] = piece
        if q < 2:
            tile_ref[:, q * BLK : (q + 1) * BLK] = piece
            for i, quarter in enumerate(quarters):
                quarter[:, q * BLK : (q + 1) * BLK] = piece[i * BLK : (i + 1) * BLK, :]


def unpack_first(view):
    def whole(*shape):
        return pl.BlockSpec(shape, lambda i: (0, 0))

    return pl.pallas_call(
        unpack_first_kernel,
        out_shape=(
            jax.ShapeDtypeStruct((TILE, HALF), F32),
            jax.ShapeDtypeStruct((TILE, TILE), F32),
        )
        + (jax.ShapeDtypeStruct((BLK, HALF), F32),) * 4,
        grid=(1,),
        in_specs=[whole(4 * TILE, BLK)],
        out_specs=(whole(TILE, HALF), whole(TILE, TILE)) + (whole(BLK, HALF),) * 4,
        name="unpack_first",
    )(view)


def unpack_rest_kernel(v_ref, *tiles):
    for i, tile in enumerate(tiles):

        @pl.when(pl.program_id(0) == i)
        def _():
            for q in range(2):
                tile[:, q * BLK : (q + 1) * BLK] = v_ref[pl.ds(q, TILE, stride=4), :]


def unpack_rest(view):
    return pl.pallas_call(
        unpack_rest_kernel,
        out_shape=(jax.ShapeDtypeStruct((TILE, HALF), F32),) * 3,
        grid=(3,),
        in_specs=[pl.BlockSpec((4 * TILE, BLK), lambda a: (a + 1, 0))],
        out_specs=(pl.BlockSpec((TILE, HALF), lambda a: (0, 0)),) * 3,
        name="unpack_rest",
    )(view)


ROWS = 256


def apply_kernel(meta, v_ref, high_ref, low_ref, noise_ref, *refs):
    held, (out_ref, real_ref, buf, sem) = refs[:8], refs[8:]
    step = pl.program_id(0)
    tile, plane, pos, core, owner = meta[step], meta[4], meta[5], meta[6], meta[7]

    def copies(i):
        return [
            pltpu.make_async_copy(held[2 * i + m], buf.at[i % 2, m], sem.at[i % 2, m]) for m in range(2)
        ]

    @pl.when(step == 0)
    def _():
        for copy in copies(0):
            copy.start()

    for i in range(4):

        @pl.when(step == i)
        def _():
            if i < 3:
                for copy in copies(i + 1):
                    copy.start()
            for copy in copies(i):
                copy.wait()

    slot = step % 2
    dims = (NN, ((), ()))

    def dot(a, b):
        return lax.dot_general(a, b, dims, preferred_element_type=F32)

    def part(at, carry):
        first = pl.multiple_of(at * ROWS, ROWS)
        rows = pl.ds(first, ROWS)
        places, values = [], []
        for m in range(2):
            for panel in range(2):
                block = 2 * panel + (core if m == 0 else 1 - core)
                places.append(pl.ds(pl.multiple_of(block * HALF, HALF), HALF))
                values.append(thirds(buf[slot, m, panel, rows, :]))
        row = (tile * ZS + plane) * TILE + first + lax.broadcasted_iota(jnp.int32, (ROWS, BLK), 0)
        lane = lax.broadcasted_iota(jnp.int32, (ROWS, BLK), 1)

        def written(half, acc):
            for q in range(2):
                there = pl.ds(4 * first + 2 * half + q, ROWS, stride=4)
                base = v_ref[there, :]
                if half == 0:
                    base = jnp.where(owner == 1, 0.0, base)
                col = (half * 32 + pos) * HALF + q * BLK + lane
                res = base - acc[:, q * BLK : (q + 1) * BLK]
                out_ref[there, :] = jnp.where(row >= col, res, 0.0)

        def summed(half):
            lanes = slice(half * HALF, (half + 1) * HALF)
            acc = None
            for here, (c0, c1, _) in zip(places, values):
                high, low = high_ref[here, lanes], low_ref[here, lanes]
                term = dot(c0, low) + dot(c1, high) + dot(c0, high)
                acc = term if acc is None else acc + term
            return acc

        written(0, summed(0))

        @pl.when(tile >= 2)
        def _():
            written(1, summed(1))

        @pl.when(tile < 2)
        def _():
            for q in range(2):
                out_ref[pl.ds(4 * first + 2 + q, ROWS, stride=4), :] = jnp.zeros((ROWS, BLK), F32)

        real = None
        for here, value in zip(places, values):
            for c in value[::-1]:
                term = dot(c, noise_ref[here, :])
                real = term if real is None else real + term
        real = real.T
        count = real_ref.shape[1]
        real_ref[0, :, rows] = real[2 * count : 3 * count] + real[count : 2 * count] + real[:count]
        return carry

    lax.fori_loop(0, TILE // ROWS, part, 0)


def apply_all(meta, view, high, low, drawn, real, held):
    wide = pl.BlockSpec((4 * TILE, BLK), lambda i, m: (m[i], 0))

    def whole(shape):
        return pl.BlockSpec(shape, lambda i, m: (0, 0))

    return pl.pallas_call(
        apply_kernel,
        out_shape=(
            jax.ShapeDtypeStruct(view.shape, F32),
            jax.ShapeDtypeStruct((4, real, TILE), F32),
        ),
        grid_spec=pltpu.PrefetchScalarGridSpec(
            num_scalar_prefetch=1,
            grid=(4,),
            in_specs=[wide, whole(high.shape), whole(low.shape), whole(drawn.shape)]
            + [pl.BlockSpec(memory_space=pl.ANY)] * len(held),
            out_specs=(wide, pl.BlockSpec((1, real, TILE), lambda i, m: (m[i], 0, 0))),
            scratch_shapes=[
                pltpu.VMEM((2, 2, 2, TILE, HALF), F32),
                pltpu.SemaphoreType.DMA((2, 2)),
            ],
        ),
        cost_estimate=pl.CostEstimate(flops=2 * 10**10, bytes_accessed=24 * 2**20, transcendentals=0),
        name="apply_all",
    )(meta, view, high, low, drawn, *held)


def lower_times(x, value):
    return jnp.concatenate([dot_nn(x[:HALF, :HALF], value[:HALF]), dot_nn(x[HALF:, :], value)], axis=0)


def upper_times(x, value):
    return jnp.concatenate([dot_tn(x[:, :HALF], value), dot_tn(x[HALF:, HALF:], value[HALF:])], axis=0)


def weights_kernel(meta, x11, x22, l21, y1, rest, noise, high_ref, low_ref, drawn_ref):
    pos, owner = meta[5], meta[7]
    y2 = lower_times(x22[...], rest[...])

    def rhs(part, at):
        ids = at + lax.broadcasted_iota(jnp.int32, (TILE, HALF), 0)
        spot = pos * HALF + lax.broadcasted_iota(jnp.int32, (TILE, HALF), 1)
        first = jnp.where(owner == 1, jnp.where(ids == spot, -1.0, 0.0), part[:, :HALF])
        return jnp.concatenate([first, part[:, HALF:], noise[:, at : at + TILE].T], axis=1)

    w2 = upper_times(x22[...], rhs(y2, TILE))
    w1 = upper_times(x11[...], rhs(y1[...], 0) - dot_tn(l21[...], w2))
    count = noise.shape[0]
    for at, value in ((0, w1), (TILE, w2)):
        here = pl.ds(at, TILE)
        high_ref[here, :], low_ref[here, :] = halves(value[:, :TILE])
        split = thirds(value[:, TILE:])
        drawn_ref[here, :] = jnp.concatenate([*split, jnp.zeros((TILE, count), jnp.bfloat16)], axis=1)


def make_weights(meta, x11, x22, l21, y1, rest, noise):
    split = jax.ShapeDtypeStruct((WIDTH, TILE), jnp.bfloat16)
    vmem = pl.BlockSpec(memory_space=pltpu.VMEM)
    return pl.pallas_call(
        weights_kernel,
        out_shape=(split, split, jax.ShapeDtypeStruct((WIDTH, 4 * noise.shape[0]), jnp.bfloat16)),
        in_specs=[pl.BlockSpec(memory_space=pltpu.SMEM)] + [vmem] * 6,
        out_specs=(vmem,) * 3,
        cost_estimate=pl.CostEstimate(flops=12 * 10**9, bytes_accessed=8 * 2**20, transcendentals=0),
        name="make_weights",
    )(meta, x11, x22, l21, y1, rest, noise)


def scattered_along_x(parts):
    got = []
    for d in (1, 2, 3):
        pairs = [((pz, 0, py, c), (pz, d, py, c)) for pz in range(ZS) for py in (0, 1) for c in range(2)]
        got.append(moved(parts[d], pairs))
    return got[0] + got[1] + got[2]


def planes(routes, value):
    return moved(
        value,
        [
            ((a, px, py, c), (b, px, py, c))
            for a, b in routes
            for px in range(XS)
            for py in range(YS)
            for c in range(2)
        ],
    )


def doubled_one(hold, z):
    got = planes(((0, 6), (1, 3)), hold)
    return jnp.where((z == 6) | (z == 3), got, hold)


def doubled_two(hold, z):
    got = planes(((0, 2), (6, 4), (1, 7), (3, 5)), hold)
    return jnp.where((z == 2) | (z == 4) | (z == 7) | (z == 5), got, hold)


def exchanged(hold, z):
    got = planes([(a, a ^ 1) for a in range(ZS)], hold)
    even = z % 2 == 0
    return jnp.where(even, hold, got), jnp.where(even, got, hold)


def square_chunks(got, y):
    arrived = [got[:32]]
    for d in (1, 2, 3):
        pairs = [
            ((pz, px, py, c), (pz, px, py + d, c)) for pz in (0, 1) for px in range(XS) for py in (0, 1) for c in range(2)
        ]
        arrived.append(moved(got[32 * d : 32 * (d + 1)], pairs))

    def picked(at):
        return jnp.where(at == 0, arrived[0], jnp.where(at == 1, arrived[1], jnp.where(at == 2, arrived[2], arrived[3])))

    return jnp.stack([picked(y), picked(jnp.mod(y - 1, YS))])


def gathered_along_y(parts, firsts, y):
    ring = [parts] + [shifted(parts, dy=d) for d in (1, 2, 3)]
    return jnp.stack(
        [turned([p[m] for p in ring], jnp.mod(y - f, YS)).reshape(128, HALF) for m, f in enumerate(firsts)]
    )


def gathered_along_x(line, x):
    ring = [line] + [shifted(line, dx=d) for d in (1, 2, 3)]
    return jnp.moveaxis(turned(ring, x), 0, 1).reshape(line.shape[0], TILE, HALF)


def y_hop(routes, value):
    return moved(
        value,
        [((pz, px, a, c), (pz, px, b, c)) for a, b in routes for pz in range(ZS) for px in range(XS) for c in range(2)],
    )


def shards(covariance, noise):
    z = lax.axis_index("row").astype(jnp.int32)
    pos = 31 - lax.axis_index("col").astype(jnp.int32)
    x, y, k = pos // 8, (pos // 2) % 4, pos % 2
    owner = (pos < 4).astype(jnp.int32)
    view = covariance.reshape(-1, BLK)
    tile0, cross, *quarters = unpack_first(view)
    meta = jnp.stack([x, jnp.mod(x + 3, XS), jnp.mod(x + 1, XS), jnp.mod(x + 2, XS), z, pos, k, owner])

    quarter = jnp.where(x == 0, quarters[0], scattered_along_x(quarters))
    others = after(quarter, *unpack_rest(view))
    hold = square_chunks(quarter, y)
    tile = jnp.where(x == 0, tile0, scattered_along_x([tile0, *others]))
    hold = doubled_one(hold, z)
    hold = doubled_two(hold, z)
    first, later = exchanged(hold, z)
    cross = after(first, cross)[0]
    cross = doubled_one(cross, z)
    line = gathered_along_y(first[:1], (0,), y)
    tile, later = after(line, tile, later)
    mine = gathered_along_x(line, x)[0]
    late_line = gathered_along_y(later, (0, 1), y)
    near = y_hop(((0, 1), (1, 0)), tile)
    away = y_hop(((0, 3), (1, 2)), tile)
    far_y = y_hop(((0, 2), (1, 3)), tile)
    other = shifted(mine, swap=1)
    other, late_line, cross = tied(other, late_line, cross)
    cross = doubled_two(cross, z)
    late = gathered_along_x(late_line, x)
    state = first_half(meta, mine, other)
    s1, s2, near, away, far_y, late, cross = tied(*state, near, away, far_y, late, cross)
    pieces = jnp.stack(
        [
            jnp.where(y == 0, tile, jnp.where(y == 1, near, jnp.where(y == 3, away, far_y))),
            jnp.where(y == 1, tile, jnp.where(y == 0, near, jnp.where(y == 2, away, far_y))),
        ]
    )
    up, down = shifted(pieces, dx=1), shifted(pieces, dx=-1)
    late_other = shifted(late, swap=1)
    c0, c1 = exchanged(cross, z)
    x11 = rest_of(s1, s2)
    x11, up, down, late_other, c0, c1 = tied(x11, up, down, late_other, c0, c1)
    far = shifted(up, dx=1)
    swaps = [shifted(value, swap=1) for value in (pieces, up, down)]
    s1, s2, l21 = second_half(meta, late, late_other, x11)
    y1 = dot_nn(x11, c0)
    rest = c1 - dot_nn(l21, y1)
    s1, s2, far = tied(s1, s2, far)
    swaps.append(shifted(far, swap=1))
    x22 = rest_of(s1, s2)
    high, low, drawn = make_weights(meta, x11, x22, l21, y1, rest, jnp.swapaxes(noise, 0, 1))
    held = [piece for pair in zip((pieces, up, down, far), swaps) for piece in pair]
    factored, real = apply_all(meta, view, high, low, drawn, noise.shape[1], held)
    return factored.reshape(covariance.shape), jnp.swapaxes(real, 1, 2)[:, None]


def solution(mesh):
    placed = (P(None, "row", None, None, "col", None), P(None, "col"))
    return jax.shard_map(
        shards,
        mesh=mesh,
        in_specs=placed,
        out_specs=(P(None, "row", None, None, "col", None), P(None, "row", None, "col")),
        check_vma=False,
    )
```

```python
import jax
import jax.numpy as jnp
from jax import lax
from jax.experimental import pallas as pl
from jax.experimental.pallas import tpu as pltpu
from jax.sharding import PartitionSpec as P


TILE = 512
HALF = 256
WIDTH = 1024
BLK = 128
SUB = 8
ZS, XS, YS = 8, 4, 4
AXES = ("row", "col")
HI = lax.Precision.HIGHEST
F32 = jnp.float32


def device_at(z, x, y, k):
    return (z % ZS) * 32 + 31 - ((((x % XS) * YS) + (y % YS)) * 2 + k)


def moved(value, pairs):
    return lax.ppermute(value, AXES, [(device_at(*a), device_at(*b)) for a, b in pairs])


def shifted(value, dz=0, dx=0, dy=0, swap=0):
    return moved(
        value,
        [
            ((z, x, y, k), (z + dz, x + dx, y + dy, k ^ swap))
            for z in range(ZS)
            for x in range(XS)
            for y in range(YS)
            for k in range(2)
        ],
    )


def turned(parts, first):
    count = len(parts)
    out = []
    for j in range(count):
        at = jnp.mod(first - j, count)
        value = parts[0]
        for i in range(1, count):
            value = jnp.where(at == i, parts[i], value)
        out.append(value)
    return jnp.stack(out)


def after(trigger, *values):
    return lax.optimization_barrier((trigger, *values))[1:]


def tied(*values):
    return lax.optimization_barrier(values)


def dot_nt(a, b):
    return lax.dot_general(a, b, (((1,), (1,)), ((), ())), precision=HI, preferred_element_type=F32)


def dot_nn(a, b):
    return lax.dot_general(a, b, (((1,), (0,)), ((), ())), precision=HI, preferred_element_type=F32)


def dot_tn(a, b):
    return lax.dot_general(a, b, (((0,), (0,)), ((), ())), precision=HI, preferred_element_type=F32)


def halves(value):
    high = value.astype(jnp.bfloat16)
    return high, (value - high.astype(F32)).astype(jnp.bfloat16)


def thirds(value):
    first, rest = value.astype(jnp.bfloat16), value
    rest = rest - first.astype(F32)
    second = rest.astype(jnp.bfloat16)
    return first, second, (rest - second.astype(F32)).astype(jnp.bfloat16)


def six_left(value):
    a, b, c = thirds(value)
    return jnp.concatenate([a, a, b, a, b, c], axis=1)


def six_right(value, axis):
    a, b, c = thirds(value)
    return jnp.concatenate([a, b, a, c, b, a], axis=axis)


def stacked(a, b, contract):
    return lax.dot_general(a, b, (contract, ((), ())), preferred_element_type=F32)


NN, NT = ((1,), (0,)), ((1,), (1,))


def eliminate(block):
    count = BLK // SUB
    s = [block[SUB * t : SUB * (t + 1), :] for t in range(count)]
    lane = lax.broadcasted_iota(jnp.int32, (SUB, BLK), 1)
    sub = lax.broadcasted_iota(jnp.int32, (SUB, BLK), 0)
    e = [(lane == sub + SUB * t).astype(F32) for t in range(count)]

    def row_of(x, i):
        return jnp.broadcast_to(x[i : i + 1, :], (SUB, BLK))

    def col_of(x, j):
        return jnp.broadcast_to(x[:, j : j + 1], (SUB, BLK))

    inverse = []
    for t in range(count):
        c = [col_of(s[t], SUB * t + j) for j in range(SUB)]
        r, x = s[t], e[t]
        ux = jnp.zeros((SUB, BLK), F32)
        dd, iv = ux, ux
        for i in range(SUB):
            p = row_of(c[i], i)
            inv = 1.0 / p
            rr, rx = row_of(r, i), row_of(x, i)
            here = sub == i
            ux = jnp.where(here, rx, ux)
            dd = jnp.where(here, p, dd)
            iv = jnp.where(here, inv, iv)
            mult = jnp.where(here, 0.0, c[i] * inv)
            for j in range(i + 1, SUB):
                c[j] = c[j] - mult * row_of(c[j], i)
            r = r - mult * rr
            x = x - mult * rx
        inverse.append(ux * lax.rsqrt(dd))
        if t + 1 < count:
            w, v = r * iv, x * iv
            wb = [row_of(w, j) for j in range(SUB)]
            vb = [row_of(v, j) for j in range(SUB)]
            for u in range(t + 1, count):
                su, eu = s[u], e[u]
                for j in range(SUB):
                    cu = col_of(s[u], SUB * t + j)
                    su = su - cu * wb[j]
                    eu = eu - cu * vb[j]
                s[u], e[u] = su, eu
    inverse = jnp.concatenate(inverse, axis=0)
    rows = lax.broadcasted_iota(jnp.int32, (BLK, BLK), 0)
    lanes = lax.broadcasted_iota(jnp.int32, (BLK, BLK), 1)
    return jnp.where(rows >= lanes, inverse, 0.0)


def eliminate_blocks(first, count, s_ref, x_ref, scratch):
    left_ref, right_ref, e_ref = scratch
    n = s_ref.shape[0]
    blocks = n // BLK

    def step(k, carry):
        at = pl.multiple_of(k * BLK, BLK)
        here = pl.ds(at, BLK)
        inv = eliminate(s_ref[here, here])
        ek = stacked(six_left(inv), six_right(x_ref[here, :], 0), NN)
        x_ref[here, :] = ek

        @pl.when(k + 1 < blocks)
        def _():
            pan = stacked(six_left(s_ref[:, here]), six_right(inv, 1), NT)
            left_ref[...] = six_left(pan)
            right_ref[...] = six_right(pan, 1)
            e_ref[...] = six_right(ek, 0)

        def under(i, inner):
            rows = pl.ds(pl.multiple_of(i * BLK, BLK), BLK)
            part = left_ref[rows, :]
            s_ref[rows, :] = s_ref[rows, :] - stacked(part, right_ref[...], NT)
            x_ref[rows, :] = x_ref[rows, :] - stacked(part, e_ref[...], NN)
            return inner

        lax.fori_loop(k + 1, blocks, under, 0)
        return carry

    lax.fori_loop(first, first + count, step, 0)


def set_identity(x_ref):
    rows = lax.broadcasted_iota(jnp.int32, x_ref.shape, 0)
    lanes = lax.broadcasted_iota(jnp.int32, x_ref.shape, 1)
    x_ref[...] = (rows == lanes).astype(F32)


def joined(core, s_ref, mine, other):
    @pl.when(core == 0)
    def _():
        s_ref[:, :HALF] = mine
        s_ref[:, HALF:] = other

    @pl.when(core == 1)
    def _():
        s_ref[:, :HALF] = other
        s_ref[:, HALF:] = mine


def first_kernel(meta, mine_ref, other_ref, s_ref, x_ref, *scratch):
    joined(meta[6], s_ref, mine_ref[...], other_ref[...])
    set_identity(x_ref)
    eliminate_blocks(0, 2, s_ref, x_ref, scratch)


def second_kernel(meta, mine_ref, other_ref, x11_ref, s_ref, x_ref, l21_ref, *scratch):
    joined(meta[6], s_ref, mine_ref[0], other_ref[0])
    l21_ref[:, :HALF] = dot_nt(s_ref[:, :HALF], x11_ref[:HALF, :HALF])
    l21_ref[:, HALF:] = dot_nt(s_ref[...], x11_ref[HALF:, :])
    joined(meta[6], s_ref, mine_ref[1], other_ref[1])
    for i in range(TILE // BLK):
        here, wide = slice(i * BLK, (i + 1) * BLK), slice(0, (i + 1) * BLK)
        s_ref[here, wide] = s_ref[here, wide] - dot_nt(l21_ref[here, :], l21_ref[wide, :])
    set_identity(x_ref)
    eliminate_blocks(0, 2, s_ref, x_ref, scratch)


def last_kernel(sin_ref, xin_ref, x_ref, s_ref, *scratch):
    s_ref[...] = sin_ref[...]
    x_ref[...] = xin_ref[...]
    eliminate_blocks(2, 2, s_ref, x_ref, scratch)


def stage(kernel, args, outs, scratch, with_meta):
    vmem = pl.BlockSpec(memory_space=pltpu.VMEM)
    specs = [pl.BlockSpec(memory_space=pltpu.SMEM)] if with_meta else []
    square = jax.ShapeDtypeStruct((TILE, TILE), F32)
    return pl.pallas_call(
        kernel,
        out_shape=(square,) * outs,
        in_specs=specs + [vmem] * (len(args) - len(specs)),
        out_specs=(vmem,) * outs,
        scratch_shapes=scratch
        + [pltpu.VMEM((TILE, 6 * BLK), jnp.bfloat16)] * 2
        + [pltpu.VMEM((6 * BLK, TILE), jnp.bfloat16)],
        cost_estimate=pl.CostEstimate(flops=2 * 10**10, bytes_accessed=4 * 2**20, transcendentals=0),
    )(*args)


def first_half(meta, mine, other):
    return stage(first_kernel, (meta, mine, other), 2, [], True)


def second_half(meta, mine, other, x11):
    return stage(second_kernel, (meta, mine, other, x11), 3, [], True)


def rest_of(s, x):
    return stage(last_kernel, (s, x), 1, [pltpu.VMEM((TILE, TILE), F32)], False)[0]


def unpack_first_kernel(v_ref, tile_ref, cross_ref, *quarters):
    for q in range(4):
        piece = v_ref[pl.ds(q, TILE, stride=4), :]
        cross_ref[:, q * BLK : (q + 1) * BLK] = piece
        if q < 2:
            tile_ref[:, q * BLK : (q + 1) * BLK] = piece
            for i, quarter in enumerate(quarters):
                quarter[:, q * BLK : (q + 1) * BLK] = piece[i * BLK : (i + 1) * BLK, :]


def unpack_first(view):
    def whole(*shape):
        return pl.BlockSpec(shape, lambda i: (0, 0))

    return pl.pallas_call(
        unpack_first_kernel,
        out_shape=(
            jax.ShapeDtypeStruct((TILE, HALF), F32),
            jax.ShapeDtypeStruct((TILE, TILE), F32),
        )
        + (jax.ShapeDtypeStruct((BLK, HALF), F32),) * 4,
        grid=(1,),
        in_specs=[whole(4 * TILE, BLK)],
        out_specs=(whole(TILE, HALF), whole(TILE, TILE)) + (whole(BLK, HALF),) * 4,
        name="unpack_first",
    )(view)


def unpack_rest_kernel(v_ref, *tiles):
    for i, tile in enumerate(tiles):

        @pl.when(pl.program_id(0) == i)
        def _():
            for q in range(2):
                tile[:, q * BLK : (q + 1) * BLK] = v_ref[pl.ds(q, TILE, stride=4), :]


def unpack_rest(view):
    return pl.pallas_call(
        unpack_rest_kernel,
        out_shape=(jax.ShapeDtypeStruct((TILE, HALF), F32),) * 3,
        grid=(3,),
        in_specs=[pl.BlockSpec((4 * TILE, BLK), lambda a: (a + 1, 0))],
        out_specs=(pl.BlockSpec((TILE, HALF), lambda a: (0, 0)),) * 3,
        name="unpack_rest",
    )(view)


ROWS = 256


def apply_kernel(meta, v_ref, high_ref, low_ref, noise_ref, *refs):
    held, (out_ref, real_ref, buf, split_ref, sem) = refs[:8], refs[8:]
    step = pl.program_id(0)
    tile, plane, pos, owner = meta[step], meta[4], meta[5], meta[7]

    def copies(i):
        return [
            pltpu.make_async_copy(held[2 * i + m], buf.at[i % 2, m], sem.at[i % 2, m]) for m in range(2)
        ]

    @pl.when(step == 0)
    def _():
        for copy in copies(0):
            copy.start()

    for i in range(4):

        @pl.when(step == i)
        def _():
            if i < 3:
                for copy in copies(i + 1):
                    copy.start()
            for copy in copies(i):
                copy.wait()

    slot = step % 2

    def part(at, carry):
        first = pl.multiple_of(at * ROWS, ROWS)
        rows = pl.ds(first, ROWS)
        for m in range(2):
            for panel in range(2):
                for i, value in enumerate(thirds(buf[slot, m, panel, rows, :])):
                    at_lane = i * WIDTH + (2 * m + panel) * HALF
                    split_ref[:, at_lane : at_lane + HALF] = value
        row = (tile * ZS + plane) * TILE + first + lax.broadcasted_iota(jnp.int32, (ROWS, BLK), 0)
        lane = lax.broadcasted_iota(jnp.int32, (ROWS, BLK), 1)

        def written(half, acc):
            for q in range(2):
                there = pl.ds(4 * first + 2 * half + q, ROWS, stride=4)
                base = v_ref[there, :]
                if half == 0:
                    base = jnp.where(owner == 1, 0.0, base)
                col = (half * 32 + pos) * HALF + q * BLK + lane
                res = base - acc[:, q * BLK : (q + 1) * BLK]
                out_ref[there, :] = jnp.where(row >= col, res, 0.0)

        def summed(half):
            lanes = slice(half * HALF, (half + 1) * HALF)
            small = stacked(split_ref[:, :WIDTH], low_ref[:, lanes], NN)
            return small + stacked(split_ref[:, : 2 * WIDTH], high_ref[:, lanes], NN)

        written(0, summed(0))

        @pl.when(tile >= 2)
        def _():
            written(1, summed(1))

        @pl.when(tile < 2)
        def _():
            for q in range(2):
                out_ref[pl.ds(4 * first + 2 + q, ROWS, stride=4), :] = jnp.zeros((ROWS, BLK), F32)

        real = stacked(split_ref[...], noise_ref[...], NN).T
        count = real_ref.shape[1]
        real_ref[0, :, rows] = real[2 * count : 3 * count] + real[count : 2 * count] + real[:count]
        return carry

    lax.fori_loop(0, TILE // ROWS, part, 0)


def apply_all(meta, view, high, low, drawn, real, held):
    wide = pl.BlockSpec((4 * TILE, BLK), lambda i, m: (m[i], 0))

    def whole(shape):
        return pl.BlockSpec(shape, lambda i, m: (0, 0))

    return pl.pallas_call(
        apply_kernel,
        out_shape=(
            jax.ShapeDtypeStruct(view.shape, F32),
            jax.ShapeDtypeStruct((4, real, TILE), F32),
        ),
        grid_spec=pltpu.PrefetchScalarGridSpec(
            num_scalar_prefetch=1,
            grid=(4,),
            in_specs=[wide, whole(high.shape), whole(low.shape), whole(drawn.shape)]
            + [pl.BlockSpec(memory_space=pl.ANY)] * len(held),
            out_specs=(wide, pl.BlockSpec((1, real, TILE), lambda i, m: (m[i], 0, 0))),
            scratch_shapes=[
                pltpu.VMEM((2, 2, 2, TILE, HALF), F32),
                pltpu.VMEM((ROWS, 3 * WIDTH), jnp.bfloat16),
                pltpu.SemaphoreType.DMA((2, 2)),
            ],
        ),
        cost_estimate=pl.CostEstimate(flops=2 * 10**10, bytes_accessed=24 * 2**20, transcendentals=0),
        name="apply_all",
    )(meta, view, high, low, drawn, *held)


def lower_times(x, value):
    return jnp.concatenate([dot_nn(x[:HALF, :HALF], value[:HALF]), dot_nn(x[HALF:, :], value)], axis=0)


def upper_times(x, value):
    return jnp.concatenate([dot_tn(x[:, :HALF], value), dot_tn(x[HALF:, HALF:], value[HALF:])], axis=0)


def weights_kernel(meta, x11, x22, l21, c0, c1, noise, high_ref, low_ref, drawn_ref):
    pos, core, owner = meta[5], meta[6], meta[7]
    y1 = lower_times(x11[...], c0[...])
    y2 = lower_times(x22[...], c1[...] - dot_nn(l21[...], y1))

    def rhs(part, at):
        ids = at + lax.broadcasted_iota(jnp.int32, (TILE, HALF), 0)
        spot = pos * HALF + lax.broadcasted_iota(jnp.int32, (TILE, HALF), 1)
        first = jnp.where(owner == 1, jnp.where(ids == spot, -1.0, 0.0), part[:, :HALF])
        return jnp.concatenate([first, part[:, HALF:], noise[:, at : at + TILE].T], axis=1)

    w2 = upper_times(x22[...], rhs(y2, TILE))
    w1 = upper_times(x11[...], rhs(y1, 0) - dot_tn(l21[...], w2))
    blank = jnp.zeros((HALF, noise.shape[0]), jnp.bfloat16)
    for panel, both in enumerate((w1, w2)):
        for half in range(2):
            at = (panel + 2 * jnp.where(core == half, 0, 1)) * HALF
            value = both[half * HALF : (half + 1) * HALF, :]
            high, low = halves(value[:, :TILE])
            drawn = jnp.concatenate([*thirds(value[:, TILE:]), blank], axis=1)
            low_ref[pl.ds(pl.multiple_of(at, HALF), HALF), :] = low
            for i in range(3):
                here = pl.ds(pl.multiple_of(i * WIDTH + at, HALF), HALF)
                drawn_ref[here, :] = drawn
                if i < 2:
                    high_ref[here, :] = high


def make_weights(meta, x11, x22, l21, c0, c1, noise):
    vmem = pl.BlockSpec(memory_space=pltpu.VMEM)
    return pl.pallas_call(
        weights_kernel,
        out_shape=(
            jax.ShapeDtypeStruct((2 * WIDTH, TILE), jnp.bfloat16),
            jax.ShapeDtypeStruct((WIDTH, TILE), jnp.bfloat16),
            jax.ShapeDtypeStruct((3 * WIDTH, 4 * noise.shape[0]), jnp.bfloat16),
        ),
        in_specs=[pl.BlockSpec(memory_space=pltpu.SMEM)] + [vmem] * 6,
        out_specs=(vmem,) * 3,
        cost_estimate=pl.CostEstimate(flops=15 * 10**9, bytes_accessed=8 * 2**20, transcendentals=0),
        name="make_weights",
    )(meta, x11, x22, l21, c0, c1, noise)


def scattered_along_x(parts):
    got = []
    for d in (1, 2, 3):
        pairs = [((pz, 0, py, c), (pz, d, py, c)) for pz in range(ZS) for py in (0, 1) for c in range(2)]
        got.append(moved(parts[d], pairs))
    return got[0] + got[1] + got[2]


def planes(routes, value):
    return moved(
        value,
        [
            ((a, px, py, c), (b, px, py, c))
            for a, b in routes
            for px in range(XS)
            for py in range(YS)
            for c in range(2)
        ],
    )


def doubled_one(hold, z):
    got = planes(((0, 6), (1, 3)), hold)
    return jnp.where((z == 6) | (z == 3), got, hold)


def doubled_two(hold, z):
    got = planes(((0, 2), (6, 4), (1, 7), (3, 5)), hold)
    return jnp.where((z == 2) | (z == 4) | (z == 7) | (z == 5), got, hold)


def exchanged(hold, z):
    got = planes([(a, a ^ 1) for a in range(ZS)], hold)
    even = z % 2 == 0
    return jnp.where(even, hold, got), jnp.where(even, got, hold)


def square_chunks(got, y):
    arrived = [got[:32]]
    for d in (1, 2, 3):
        pairs = [
            ((pz, px, py, c), (pz, px, py + d, c)) for pz in (0, 1) for px in range(XS) for py in (0, 1) for c in range(2)
        ]
        arrived.append(moved(got[32 * d : 32 * (d + 1)], pairs))

    def picked(at):
        return jnp.where(at == 0, arrived[0], jnp.where(at == 1, arrived[1], jnp.where(at == 2, arrived[2], arrived[3])))

    return jnp.stack([picked(y), picked(jnp.mod(y - 1, YS))])


def gathered_along_y(parts, firsts, y):
    ring = [parts] + [shifted(parts, dy=d) for d in (1, 2, 3)]
    return jnp.stack(
        [turned([p[m] for p in ring], jnp.mod(y - f, YS)).reshape(128, HALF) for m, f in enumerate(firsts)]
    )


def gathered_along_x(line, x):
    ring = [line] + [shifted(line, dx=d) for d in (1, 2, 3)]
    return jnp.moveaxis(turned(ring, x), 0, 1).reshape(line.shape[0], TILE, HALF)


def y_hop(routes, value):
    return moved(
        value,
        [((pz, px, a, c), (pz, px, b, c)) for a, b in routes for pz in range(ZS) for px in range(XS) for c in range(2)],
    )


def shards(covariance, noise):
    z = lax.axis_index("row").astype(jnp.int32)
    pos = 31 - lax.axis_index("col").astype(jnp.int32)
    x, y, k = pos // 8, (pos // 2) % 4, pos % 2
    owner = (pos < 4).astype(jnp.int32)
    view = covariance.reshape(-1, BLK)
    tile0, cross, *quarters = unpack_first(view)
    meta = jnp.stack([x, jnp.mod(x + 3, XS), jnp.mod(x + 1, XS), jnp.mod(x + 2, XS), z, pos, k, owner])

    quarter = jnp.where(x == 0, quarters[0], scattered_along_x(quarters))
    others = after(quarter, *unpack_rest(view))
    hold = square_chunks(quarter, y)
    tile = jnp.where(x == 0, tile0, scattered_along_x([tile0, *others]))
    hold = doubled_one(hold, z)
    hold = doubled_two(hold, z)
    first, later = exchanged(hold, z)
    cross = after(first, cross)[0]
    cross = doubled_one(cross, z)
    line = gathered_along_y(first[:1], (0,), y)
    tile, later = after(line, tile, later)
    mine = gathered_along_x(line, x)[0]
    late_line = gathered_along_y(later, (0, 1), y)
    near = y_hop(((0, 1), (1, 0)), tile)
    away = y_hop(((0, 3), (1, 2)), tile)
    far_y = y_hop(((0, 2), (1, 3)), tile)
    other = shifted(mine, swap=1)
    other, late_line, cross = tied(other, late_line, cross)
    cross = doubled_two(cross, z)
    late = gathered_along_x(late_line, x)
    state = first_half(meta, mine, other)
    s1, s2, near, away, far_y, late = tied(*state, near, away, far_y, late)
    pieces = jnp.stack(
        [
            jnp.where(y == 0, tile, jnp.where(y == 1, near, jnp.where(y == 3, away, far_y))),
            jnp.where(y == 1, tile, jnp.where(y == 0, near, jnp.where(y == 2, away, far_y))),
        ]
    )
    up, down = shifted(pieces, dx=1), shifted(pieces, dx=-1)
    late_other = shifted(late, swap=1)
    x11 = rest_of(s1, s2)
    x11, up, down, late_other, cross = tied(x11, up, down, late_other, cross)
    c0, c1 = exchanged(cross, z)
    far = shifted(up, dx=1)
    swaps = [shifted(value, swap=1) for value in (pieces, up, down)]
    s1, s2, l21 = second_half(meta, late, late_other, x11)
    s1, s2, far = tied(s1, s2, far)
    swaps.append(shifted(far, swap=1))
    x22 = rest_of(s1, s2)
    high, low, drawn = make_weights(meta, x11, x22, l21, c0, c1, jnp.swapaxes(noise, 0, 1))
    held = [piece for pair in zip((pieces, up, down, far), swaps) for piece in pair]
    factored, real = apply_all(meta, view, high, low, drawn, noise.shape[1], held)
    return factored.reshape(covariance.shape), jnp.swapaxes(real, 1, 2)[:, None]


def solution(mesh):
    placed = (P(None, "row", None, None, "col", None), P(None, "col"))
    return jax.shard_map(
        shards,
        mesh=mesh,
        in_specs=placed,
        out_specs=(P(None, "row", None, None, "col", None), P(None, "row", None, "col")),
        check_vma=False,
    )
```

```python
import jax
import jax.numpy as jnp
from jax import lax
from jax.experimental import pallas as pl
from jax.experimental.pallas import tpu as pltpu
from jax.sharding import PartitionSpec as P


TILE = 512
HALF = 256
WIDTH = 1024
BLK = 128
SUB = 8
ZS, XS, YS = 8, 4, 4
AXES = ("row", "col")
HI = lax.Precision.HIGHEST
F32 = jnp.float32


def device_at(z, x, y, k):
    return (z % ZS) * 32 + 31 - ((((x % XS) * YS) + (y % YS)) * 2 + k)


def moved(value, pairs):
    return lax.ppermute(value, AXES, [(device_at(*a), device_at(*b)) for a, b in pairs])


def shifted(value, dz=0, dx=0, dy=0, swap=0):
    return moved(
        value,
        [
            ((z, x, y, k), (z + dz, x + dx, y + dy, k ^ swap))
            for z in range(ZS)
            for x in range(XS)
            for y in range(YS)
            for k in range(2)
        ],
    )


def turned(parts, first):
    count = len(parts)
    out = []
    for j in range(count):
        at = jnp.mod(first - j, count)
        value = parts[0]
        for i in range(1, count):
            value = jnp.where(at == i, parts[i], value)
        out.append(value)
    return jnp.stack(out)


def after(trigger, *values):
    return lax.optimization_barrier((trigger, *values))[1:]


def tied(*values):
    return lax.optimization_barrier(values)


def dot_nt(a, b):
    return lax.dot_general(a, b, (((1,), (1,)), ((), ())), precision=HI, preferred_element_type=F32)


def dot_nn(a, b):
    return lax.dot_general(a, b, (((1,), (0,)), ((), ())), precision=HI, preferred_element_type=F32)


def dot_tn(a, b):
    return lax.dot_general(a, b, (((0,), (0,)), ((), ())), precision=HI, preferred_element_type=F32)


def halves(value):
    high = value.astype(jnp.bfloat16)
    return high, (value - high.astype(F32)).astype(jnp.bfloat16)


def thirds(value):
    first, rest = value.astype(jnp.bfloat16), value
    rest = rest - first.astype(F32)
    second = rest.astype(jnp.bfloat16)
    return first, second, (rest - second.astype(F32)).astype(jnp.bfloat16)


def six_left(value):
    a, b, c = thirds(value)
    return jnp.concatenate([a, a, b, a, b, c], axis=1)


def six_right(value, axis):
    a, b, c = thirds(value)
    return jnp.concatenate([a, b, a, c, b, a], axis=axis)


def stacked(a, b, contract):
    return lax.dot_general(a, b, (contract, ((), ())), preferred_element_type=F32)


NN, NT = ((1,), (0,)), ((1,), (1,))


def eliminate(block):
    count = BLK // SUB
    s = [block[SUB * t : SUB * (t + 1), :] for t in range(count)]
    lane = lax.broadcasted_iota(jnp.int32, (SUB, BLK), 1)
    sub = lax.broadcasted_iota(jnp.int32, (SUB, BLK), 0)
    e = [(lane == sub + SUB * t).astype(F32) for t in range(count)]

    def row_of(x, i):
        return jnp.broadcast_to(x[i : i + 1, :], (SUB, BLK))

    def col_of(x, j):
        return jnp.broadcast_to(x[:, j : j + 1], (SUB, BLK))

    inverse = []
    for t in range(count):
        c = [col_of(s[t], SUB * t + j) for j in range(SUB)]
        r, x = s[t], e[t]
        ux = jnp.zeros((SUB, BLK), F32)
        dd = ux
        for i in range(0, SUB, 2):
            a, b = row_of(c[i], i), row_of(c[i], i + 1)
            d = row_of(c[i + 1], i + 1)
            ra, rb = row_of(r, i), row_of(r, i + 1)
            xa, xb = row_of(x, i), row_of(x, i + 1)
            det = a * d - b * b
            inv = 1.0 / det
            ratio = b / a
            ux = jnp.where(sub == i, xa, jnp.where(sub == i + 1, xb - ratio * xa, ux))
            dd = jnp.where(sub == i, a, jnp.where(sub == i + 1, d - ratio * b, dd))
            pair = (sub == i) | (sub == i + 1)
            ca, cb = c[i], c[i + 1]
            ma = jnp.where(sub == i, -d, jnp.where(sub == i + 1, b, ca * d - cb * b)) * inv
            mb = jnp.where(sub == i, b, jnp.where(sub == i + 1, -a, cb * a - ca * b)) * inv
            r = jnp.where(pair, 0.0, r) - (ma * ra + mb * rb)
            x = jnp.where(pair, 0.0, x) - (ma * xa + mb * xb)
            for j in range(i + 2, SUB):
                c[j] = jnp.where(pair, 0.0, c[j]) - (ma * row_of(c[j], i) + mb * row_of(c[j], i + 1))
        inverse.append(ux * lax.rsqrt(dd))
        if t + 1 < count:
            wb = [row_of(r, j) for j in range(SUB)]
            vb = [row_of(x, j) for j in range(SUB)]
            for u in range(t + 1, count):
                su, eu = s[u], e[u]
                for j in range(SUB):
                    cu = col_of(s[u], SUB * t + j)
                    su = su - cu * wb[j]
                    eu = eu - cu * vb[j]
                s[u], e[u] = su, eu
    inverse = jnp.concatenate(inverse, axis=0)
    rows = lax.broadcasted_iota(jnp.int32, (BLK, BLK), 0)
    lanes = lax.broadcasted_iota(jnp.int32, (BLK, BLK), 1)
    return jnp.where(rows >= lanes, inverse, 0.0)


def eliminate_blocks(first, count, s_ref, x_ref, scratch):
    left_ref, right_ref, e_ref = scratch
    n = s_ref.shape[0]
    blocks = n // BLK

    def step(k, carry):
        at = pl.multiple_of(k * BLK, BLK)
        here = pl.ds(at, BLK)
        inv = eliminate(s_ref[here, here])
        ek = stacked(six_left(inv), six_right(x_ref[here, :], 0), NN)
        x_ref[here, :] = ek

        @pl.when(k + 1 < blocks)
        def _():
            pan = stacked(six_left(s_ref[:, here]), six_right(inv, 1), NT)
            left_ref[...] = six_left(pan)
            right_ref[...] = six_right(pan, 1)
            e_ref[...] = six_right(ek, 0)

        def under(i, inner):
            rows = pl.ds(pl.multiple_of(i * BLK, BLK), BLK)
            part = left_ref[rows, :]
            s_ref[rows, :] = s_ref[rows, :] - stacked(part, right_ref[...], NT)
            x_ref[rows, :] = x_ref[rows, :] - stacked(part, e_ref[...], NN)
            return inner

        lax.fori_loop(k + 1, blocks, under, 0)
        return carry

    lax.fori_loop(first, first + count, step, 0)


def set_identity(x_ref):
    rows = lax.broadcasted_iota(jnp.int32, x_ref.shape, 0)
    lanes = lax.broadcasted_iota(jnp.int32, x_ref.shape, 1)
    x_ref[...] = (rows == lanes).astype(F32)


def joined(core, s_ref, mine, other):
    @pl.when(core == 0)
    def _():
        s_ref[:, :HALF] = mine
        s_ref[:, HALF:] = other

    @pl.when(core == 1)
    def _():
        s_ref[:, :HALF] = other
        s_ref[:, HALF:] = mine


def first_kernel(meta, mine_ref, other_ref, x_ref, s_ref, *scratch):
    joined(meta[6], s_ref, mine_ref[...], other_ref[...])
    set_identity(x_ref)
    eliminate_blocks(0, 4, s_ref, x_ref, scratch)


def second_kernel(meta, mine_ref, other_ref, x11_ref, x_ref, l21_ref, s_ref, *scratch):
    joined(meta[6], s_ref, mine_ref[0], other_ref[0])

    def solve(i, carry):
        here = pl.ds(pl.multiple_of(i * BLK, BLK), BLK)
        l21_ref[here, :] = dot_nt(s_ref[here, :], x11_ref[...])
        return carry

    lax.fori_loop(0, TILE // BLK, solve, 0)
    joined(meta[6], s_ref, mine_ref[1], other_ref[1])

    def update(i, carry):
        here = pl.ds(pl.multiple_of(i * BLK, BLK), BLK)
        s_ref[here, :] = s_ref[here, :] - dot_nt(l21_ref[here, :], l21_ref[...])
        return carry

    lax.fori_loop(0, TILE // BLK, update, 0)
    set_identity(x_ref)
    eliminate_blocks(0, 4, s_ref, x_ref, scratch)


def stage(kernel, args, outs, scratch, with_meta):
    vmem = pl.BlockSpec(memory_space=pltpu.VMEM)
    specs = [pl.BlockSpec(memory_space=pltpu.SMEM)] if with_meta else []
    square = jax.ShapeDtypeStruct((TILE, TILE), F32)
    return pl.pallas_call(
        kernel,
        out_shape=(square,) * outs,
        in_specs=specs + [vmem] * (len(args) - len(specs)),
        out_specs=(vmem,) * outs,
        scratch_shapes=scratch
        + [pltpu.VMEM((TILE, 6 * BLK), jnp.bfloat16)] * 2
        + [pltpu.VMEM((6 * BLK, TILE), jnp.bfloat16)],
        cost_estimate=pl.CostEstimate(flops=2 * 10**10, bytes_accessed=4 * 2**20, transcendentals=0),
    )(*args)


def first_factor(meta, mine, other):
    return stage(first_kernel, (meta, mine, other), 1, [pltpu.VMEM((TILE, TILE), F32)], True)[0]


def second_all(meta, mine, other, x11):
    args = (meta, mine, other, x11)
    return stage(second_kernel, args, 2, [pltpu.VMEM((TILE, TILE), F32)], True)


def unpack_first_kernel(v_ref, tile_ref, cross_ref, *quarters):
    for q in range(4):
        piece = v_ref[pl.ds(q, TILE, stride=4), :]
        cross_ref[:, q * BLK : (q + 1) * BLK] = piece
        if q < 2:
            tile_ref[:, q * BLK : (q + 1) * BLK] = piece
            for i, quarter in enumerate(quarters):
                quarter[:, q * BLK : (q + 1) * BLK] = piece[i * BLK : (i + 1) * BLK, :]


def unpack_first(view):
    def whole(*shape):
        return pl.BlockSpec(shape, lambda i: (0, 0))

    return pl.pallas_call(
        unpack_first_kernel,
        out_shape=(
            jax.ShapeDtypeStruct((TILE, HALF), F32),
            jax.ShapeDtypeStruct((TILE, TILE), F32),
        )
        + (jax.ShapeDtypeStruct((BLK, HALF), F32),) * 4,
        grid=(1,),
        in_specs=[whole(4 * TILE, BLK)],
        out_specs=(whole(TILE, HALF), whole(TILE, TILE)) + (whole(BLK, HALF),) * 4,
        name="unpack_first",
    )(view)


def unpack_rest_kernel(v_ref, *tiles):
    for i, tile in enumerate(tiles):

        @pl.when(pl.program_id(0) == i)
        def _():
            for q in range(2):
                tile[:, q * BLK : (q + 1) * BLK] = v_ref[pl.ds(q, TILE, stride=4), :]


def unpack_rest(view):
    return pl.pallas_call(
        unpack_rest_kernel,
        out_shape=(jax.ShapeDtypeStruct((TILE, HALF), F32),) * 3,
        grid=(3,),
        in_specs=[pl.BlockSpec((4 * TILE, BLK), lambda a: (a + 1, 0))],
        out_specs=(pl.BlockSpec((TILE, HALF), lambda a: (0, 0)),) * 3,
        name="unpack_rest",
    )(view)


ROWS = 256


def apply_kernel(meta, v_ref, high_ref, low_ref, noise_ref, *refs):
    held, (out_ref, real_ref, buf, split_ref, sem) = refs[:10], refs[10:]
    step = pl.program_id(0)
    tile, plane, pos, owner = meta[step], meta[4], meta[5], meta[7]

    def copies(i):
        spots = [(m, panel) for m in range(2) for panel in range(2)]
        if i < 3:
            sources = [held[2 * i + m].at[panel] for m, panel in spots]
        else:
            sources = [held[6 + 2 * m + panel] for m, panel in spots]
        return [
            pltpu.make_async_copy(source, buf.at[i % 2, m, panel], sem.at[i % 2, m, panel])
            for source, (m, panel) in zip(sources, spots)
        ]

    @pl.when(step == 0)
    def _():
        for copy in copies(0):
            copy.start()

    for i in range(4):

        @pl.when(step == i)
        def _():
            if i < 3:
                for copy in copies(i + 1):
                    copy.start()
            for copy in copies(i):
                copy.wait()

    slot = step % 2

    def part(at, carry):
        first = pl.multiple_of(at * ROWS, ROWS)
        rows = pl.ds(first, ROWS)
        for m in range(2):
            for panel in range(2):
                for i, value in enumerate(thirds(buf[slot, m, panel, rows, :])):
                    at_lane = i * WIDTH + (2 * m + panel) * HALF
                    split_ref[:, at_lane : at_lane + HALF] = value
        row = (tile * ZS + plane) * TILE + first + lax.broadcasted_iota(jnp.int32, (ROWS, BLK), 0)
        lane = lax.broadcasted_iota(jnp.int32, (ROWS, BLK), 1)

        def written(half, acc):
            for q in range(2):
                there = pl.ds(4 * first + 2 * half + q, ROWS, stride=4)
                base = v_ref[there, :]
                if half == 0:
                    base = jnp.where(owner == 1, 0.0, base)
                col = (half * 32 + pos) * HALF + q * BLK + lane
                res = base - acc[:, q * BLK : (q + 1) * BLK]
                out_ref[there, :] = jnp.where(row >= col, res, 0.0)

        def summed(half):
            lanes = slice(half * HALF, (half + 1) * HALF)
            small = stacked(split_ref[:, :WIDTH], low_ref[:, lanes], NN)
            return small + stacked(split_ref[:, : 2 * WIDTH], high_ref[:, lanes], NN)

        written(0, summed(0))

        @pl.when(tile >= 2)
        def _():
            written(1, summed(1))

        @pl.when(tile < 2)
        def _():
            for q in range(2):
                out_ref[pl.ds(4 * first + 2 + q, ROWS, stride=4), :] = jnp.zeros((ROWS, BLK), F32)

        real = stacked(split_ref[...], noise_ref[...], NN).T
        count = real_ref.shape[1]
        real_ref[0, :, rows] = real[2 * count : 3 * count] + real[count : 2 * count] + real[:count]
        return carry

    lax.fori_loop(0, TILE // ROWS, part, 0)


def apply_all(meta, view, high, low, drawn, real, held):
    wide = pl.BlockSpec((4 * TILE, BLK), lambda i, m: (m[i], 0))

    def whole(shape):
        return pl.BlockSpec(shape, lambda i, m: (0, 0))

    return pl.pallas_call(
        apply_kernel,
        out_shape=(
            jax.ShapeDtypeStruct(view.shape, F32),
            jax.ShapeDtypeStruct((4, real, TILE), F32),
        ),
        grid_spec=pltpu.PrefetchScalarGridSpec(
            num_scalar_prefetch=1,
            grid=(4,),
            in_specs=[wide, whole(high.shape), whole(low.shape), whole(drawn.shape)]
            + [pl.BlockSpec(memory_space=pl.ANY)] * len(held),
            out_specs=(wide, pl.BlockSpec((1, real, TILE), lambda i, m: (m[i], 0, 0))),
            scratch_shapes=[
                pltpu.VMEM((2, 2, 2, TILE, HALF), F32),
                pltpu.VMEM((ROWS, 3 * WIDTH), jnp.bfloat16),
                pltpu.SemaphoreType.DMA((2, 2, 2)),
            ],
        ),
        cost_estimate=pl.CostEstimate(flops=2 * 10**10, bytes_accessed=24 * 2**20, transcendentals=0),
        name="apply_all",
    )(meta, view, high, low, drawn, *held)


def by_rows(body):
    def step(i, carry):
        body(pl.ds(pl.multiple_of(i * BLK, BLK), BLK))
        return carry

    lax.fori_loop(0, TILE // BLK, step, 0)


def weights_kernel(meta, x11, x22, l21, c0, c1, noise, high_ref, low_ref, drawn_ref, top, bottom, w1_ref, w2_ref):
    pos, core, owner = meta[5], meta[6], meta[7]
    cols = slice(0, TILE)

    def first_solve(rows):
        top[rows, cols] = dot_nn(x11[rows, :], c0[...])

    def reduced(rows):
        w1_ref[rows, cols] = c1[rows, :] - dot_nn(l21[rows, :], top[:, cols])

    def second_solve(rows):
        bottom[rows, cols] = dot_nn(x22[rows, :], w1_ref[:, cols])

    by_rows(first_solve)
    by_rows(reduced)
    by_rows(second_solve)
    for ref, at in ((top, 0), (bottom, TILE)):
        ref[:, TILE:] = noise[:, at : at + TILE].T

        @pl.when(owner == 1)
        def _():
            ids = at + lax.broadcasted_iota(jnp.int32, (TILE, HALF), 0)
            spot = pos * HALF + lax.broadcasted_iota(jnp.int32, (TILE, HALF), 1)
            ref[:, :HALF] = jnp.where(ids == spot, -1.0, 0.0)

    def second_back(rows):
        w2_ref[rows, :] = dot_tn(x22[:, rows], bottom[...])

    def top_reduced(rows):
        top[rows, :] = top[rows, :] - dot_tn(l21[:, rows], w2_ref[...])

    def first_back(rows):
        w1_ref[rows, :] = dot_tn(x11[:, rows], top[...])

    by_rows(second_back)
    by_rows(top_reduced)
    by_rows(first_back)
    w1, w2 = w1_ref, w2_ref
    blank = jnp.zeros((HALF, noise.shape[0]), jnp.bfloat16)
    for panel, both in enumerate((w1, w2)):
        for half in range(2):
            at = (panel + 2 * jnp.where(core == half, 0, 1)) * HALF
            value = both[half * HALF : (half + 1) * HALF, :]
            high, low = halves(value[:, :TILE])
            drawn = jnp.concatenate([*thirds(value[:, TILE:]), blank], axis=1)
            low_ref[pl.ds(pl.multiple_of(at, HALF), HALF), :] = low
            for i in range(3):
                here = pl.ds(pl.multiple_of(i * WIDTH + at, HALF), HALF)
                drawn_ref[here, :] = drawn
                if i < 2:
                    high_ref[here, :] = high


def make_weights(meta, x11, x22, l21, c0, c1, noise):
    vmem = pl.BlockSpec(memory_space=pltpu.VMEM)
    return pl.pallas_call(
        weights_kernel,
        out_shape=(
            jax.ShapeDtypeStruct((2 * WIDTH, TILE), jnp.bfloat16),
            jax.ShapeDtypeStruct((WIDTH, TILE), jnp.bfloat16),
            jax.ShapeDtypeStruct((3 * WIDTH, 4 * noise.shape[0]), jnp.bfloat16),
        ),
        in_specs=[pl.BlockSpec(memory_space=pltpu.SMEM)] + [vmem] * 6,
        out_specs=(vmem,) * 3,
        scratch_shapes=[pltpu.VMEM((TILE, TILE + noise.shape[0]), F32)] * 4,
        cost_estimate=pl.CostEstimate(flops=15 * 10**9, bytes_accessed=8 * 2**20, transcendentals=0),
        name="make_weights",
    )(meta, x11, x22, l21, c0, c1, noise)


def scattered_along_x(parts):
    got = []
    for d in (1, 2, 3):
        pairs = [((pz, 0, py, c), (pz, d, py, c)) for pz in range(ZS) for py in (0, 1) for c in range(2)]
        got.append(moved(parts[d], pairs))
    return got[0] + got[1] + got[2]


def planes(routes, value):
    return moved(
        value,
        [
            ((a, px, py, c), (b, px, py, c))
            for a, b in routes
            for px in range(XS)
            for py in range(YS)
            for c in range(2)
        ],
    )


def doubled_one(hold, z):
    got = planes(((0, 6), (1, 3)), hold)
    return jnp.where((z == 6) | (z == 3), got, hold)


def doubled_two(hold, z):
    got = planes(((0, 2), (6, 4), (1, 7), (3, 5)), hold)
    return jnp.where((z == 2) | (z == 4) | (z == 7) | (z == 5), got, hold)


def exchanged(hold, z):
    got = planes([(a, a ^ 1) for a in range(ZS)], hold)
    even = z % 2 == 0
    return jnp.where(even, hold, got), jnp.where(even, got, hold)


def square_chunks(got, y):
    arrived = [got[:32]]
    for d in (1, 2, 3):
        pairs = [
            ((pz, px, py, c), (pz, px, py + d, c)) for pz in (0, 1) for px in range(XS) for py in (0, 1) for c in range(2)
        ]
        arrived.append(moved(got[32 * d : 32 * (d + 1)], pairs))

    def picked(at):
        return jnp.where(at == 0, arrived[0], jnp.where(at == 1, arrived[1], jnp.where(at == 2, arrived[2], arrived[3])))

    return jnp.stack([picked(y), picked(jnp.mod(y - 1, YS))])


def gathered_along_y(parts, firsts, y):
    ring = [parts] + [shifted(parts, dy=d) for d in (1, 2, 3)]
    return jnp.stack(
        [turned([p[m] for p in ring], jnp.mod(y - f, YS)).reshape(128, HALF) for m, f in enumerate(firsts)]
    )


def gathered_along_x(line, x):
    ring = [line] + [shifted(line, dx=d) for d in (1, 2, 3)]
    return jnp.moveaxis(turned(ring, x), 0, 1).reshape(line.shape[0], TILE, HALF)


def y_hop(routes, value):
    return moved(
        value,
        [((pz, px, a, c), (pz, px, b, c)) for a, b in routes for pz in range(ZS) for px in range(XS) for c in range(2)],
    )


def shards(covariance, noise):
    z = lax.axis_index("row").astype(jnp.int32)
    pos = 31 - lax.axis_index("col").astype(jnp.int32)
    x, y, k = pos // 8, (pos // 2) % 4, pos % 2
    owner = (pos < 4).astype(jnp.int32)
    view = covariance.reshape(-1, BLK)
    tile0, cross, *quarters = unpack_first(view)
    meta = jnp.stack([x, jnp.mod(x + 3, XS), jnp.mod(x + 1, XS), jnp.mod(x + 2, XS), z, pos, k, owner])

    quarter = jnp.where(x == 0, quarters[0], scattered_along_x(quarters))
    others = after(quarter, *unpack_rest(view))
    hold = square_chunks(quarter, y)
    tile = jnp.where(x == 0, tile0, scattered_along_x([tile0, *others]))
    hold = doubled_one(hold, z)
    hold = doubled_two(hold, z)
    first, later = exchanged(hold, z)
    cross = after(first, cross)[0]
    cross = doubled_one(cross, z)
    line = gathered_along_y(first[:1], (0,), y)
    tile, later = after(line, tile, later)
    mine = gathered_along_x(line, x)[0]
    late_line = gathered_along_y(later, (0, 1), y)
    near = y_hop(((0, 1), (1, 0)), tile)
    away = y_hop(((0, 3), (1, 2)), tile)
    far_y = y_hop(((0, 2), (1, 3)), tile)
    other = shifted(mine, swap=1)
    other, late_line, cross = tied(other, late_line, cross)
    cross = doubled_two(cross, z)
    late = gathered_along_x(late_line, x)
    x11 = first_factor(meta, mine, other)
    x11, near, away, far_y, late, cross = tied(x11, near, away, far_y, late, cross)
    late_other = shifted(late, swap=1)
    pieces = jnp.stack(
        [
            jnp.where(y == 0, tile, jnp.where(y == 1, near, jnp.where(y == 3, away, far_y))),
            jnp.where(y == 1, tile, jnp.where(y == 0, near, jnp.where(y == 2, away, far_y))),
        ]
    )
    up, down = shifted(pieces, dx=1), shifted(pieces, dx=-1)
    c0, c1 = exchanged(cross, z)
    swaps = [shifted(pieces, swap=1)]
    x22, l21 = second_all(meta, late, late_other, x11)
    x22, up, down = tied(x22, up, down)
    far0, far1 = shifted(down[0], dx=-1), shifted(up[1], dx=1)
    swaps += [shifted(up, swap=1), shifted(down, swap=1)]
    high, low, drawn = make_weights(meta, x11, x22, l21, c0, c1, jnp.swapaxes(noise, 0, 1))
    high, far0, far1 = tied(high, far0, far1)
    held = [piece for pair in zip((pieces, up, down), swaps) for piece in pair]
    held += [far0, far1, shifted(far0, swap=1), shifted(far1, swap=1)]
    factored, real = apply_all(meta, view, high, low, drawn, noise.shape[1], held)
    return factored.reshape(covariance.shape), jnp.swapaxes(real, 1, 2)[:, None]


def solution(mesh):
    placed = (P(None, "row", None, None, "col", None), P(None, "col"))
    return jax.shard_map(
        shards,
        mesh=mesh,
        in_specs=placed,
        out_specs=(P(None, "row", None, None, "col", None), P(None, "row", None, "col")),
        check_vma=False,
    )
```

```python
import jax
import jax.numpy as jnp
from jax import lax
from jax.experimental import pallas as pl
from jax.experimental.pallas import tpu as pltpu
from jax.sharding import PartitionSpec as P


TILE = 512
HALF = 256
WIDTH = 1024
BLK = 128
SUB = 8
ZS, XS, YS = 8, 4, 4
AXES = ("row", "col")
HI = lax.Precision.HIGHEST
F32 = jnp.float32


def device_at(z, x, y, k):
    return (z % ZS) * 32 + 31 - ((((x % XS) * YS) + (y % YS)) * 2 + k)


def moved(value, pairs):
    return lax.ppermute(value, AXES, [(device_at(*a), device_at(*b)) for a, b in pairs])


def shifted(value, dz=0, dx=0, dy=0, swap=0):
    return moved(
        value,
        [
            ((z, x, y, k), (z + dz, x + dx, y + dy, k ^ swap))
            for z in range(ZS)
            for x in range(XS)
            for y in range(YS)
            for k in range(2)
        ],
    )


def turned(parts, first):
    count = len(parts)
    out = []
    for j in range(count):
        at = jnp.mod(first - j, count)
        value = parts[0]
        for i in range(1, count):
            value = jnp.where(at == i, parts[i], value)
        out.append(value)
    return jnp.stack(out)


def after(trigger, *values):
    return lax.optimization_barrier((trigger, *values))[1:]


def tied(*values):
    return lax.optimization_barrier(values)


def dot_nt(a, b):
    return lax.dot_general(a, b, (((1,), (1,)), ((), ())), precision=HI, preferred_element_type=F32)


def dot_nn(a, b):
    return lax.dot_general(a, b, (((1,), (0,)), ((), ())), precision=HI, preferred_element_type=F32)


def dot_tn(a, b):
    return lax.dot_general(a, b, (((0,), (0,)), ((), ())), precision=HI, preferred_element_type=F32)


def halves(value):
    high = value.astype(jnp.bfloat16)
    return high, (value - high.astype(F32)).astype(jnp.bfloat16)


def thirds(value):
    first, rest = value.astype(jnp.bfloat16), value
    rest = rest - first.astype(F32)
    second = rest.astype(jnp.bfloat16)
    return first, second, (rest - second.astype(F32)).astype(jnp.bfloat16)


def six_left(value):
    a, b, c = thirds(value)
    return jnp.concatenate([a, a, b, a, b, c], axis=1)


def six_right(value, axis):
    a, b, c = thirds(value)
    return jnp.concatenate([a, b, a, c, b, a], axis=axis)


def stacked(a, b, contract):
    return lax.dot_general(a, b, (contract, ((), ())), preferred_element_type=F32)


NN, NT = ((1,), (0,)), ((1,), (1,))


def eliminate(block):
    count = BLK // SUB
    s = [block[SUB * t : SUB * (t + 1), :] for t in range(count)]
    lane = lax.broadcasted_iota(jnp.int32, (SUB, BLK), 1)
    sub = lax.broadcasted_iota(jnp.int32, (SUB, BLK), 0)
    e = [(lane == sub + SUB * t).astype(F32) for t in range(count)]

    def row_of(x, i):
        return jnp.broadcast_to(x[i : i + 1, :], (SUB, BLK))

    def col_of(x, j):
        return jnp.broadcast_to(x[:, j : j + 1], (SUB, BLK))

    inverse = []
    for t in range(count):
        c = [col_of(s[t], SUB * t + j) for j in range(SUB)]
        r, x = s[t], e[t]
        ux = jnp.zeros((SUB, BLK), F32)
        dd = ux
        for i in range(0, SUB, 2):
            a, b = row_of(c[i], i), row_of(c[i], i + 1)
            d = row_of(c[i + 1], i + 1)
            ra, rb = row_of(r, i), row_of(r, i + 1)
            xa, xb = row_of(x, i), row_of(x, i + 1)
            det = a * d - b * b
            inv = 1.0 / det
            ratio = b / a
            ux = jnp.where(sub == i, xa, jnp.where(sub == i + 1, xb - ratio * xa, ux))
            dd = jnp.where(sub == i, a, jnp.where(sub == i + 1, d - ratio * b, dd))
            pair = (sub == i) | (sub == i + 1)
            ca, cb = c[i], c[i + 1]
            ma = jnp.where(sub == i, -d, jnp.where(sub == i + 1, b, ca * d - cb * b)) * inv
            mb = jnp.where(sub == i, b, jnp.where(sub == i + 1, -a, cb * a - ca * b)) * inv
            r = jnp.where(pair, 0.0, r) - (ma * ra + mb * rb)
            x = jnp.where(pair, 0.0, x) - (ma * xa + mb * xb)
            for j in range(i + 2, SUB):
                c[j] = jnp.where(pair, 0.0, c[j]) - (ma * row_of(c[j], i) + mb * row_of(c[j], i + 1))
        inverse.append(ux * lax.rsqrt(dd))
        if t + 1 < count:
            wb = [row_of(r, j) for j in range(SUB)]
            vb = [row_of(x, j) for j in range(SUB)]
            for u in range(t + 1, count):
                su, eu = s[u], e[u]
                for j in range(SUB):
                    cu = col_of(s[u], SUB * t + j)
                    su = su - cu * wb[j]
                    eu = eu - cu * vb[j]
                s[u], e[u] = su, eu
    inverse = jnp.concatenate(inverse, axis=0)
    rows = lax.broadcasted_iota(jnp.int32, (BLK, BLK), 0)
    lanes = lax.broadcasted_iota(jnp.int32, (BLK, BLK), 1)
    return jnp.where(rows >= lanes, inverse, 0.0)


def eliminate_blocks(first, count, s_ref, x_ref, scratch):
    left_ref, right_ref, e_ref = scratch
    n = s_ref.shape[0]
    blocks = n // BLK

    def step(k, carry):
        at = pl.multiple_of(k * BLK, BLK)
        here = pl.ds(at, BLK)
        inv = eliminate(s_ref[here, here])
        ek = stacked(six_left(inv), six_right(x_ref[here, :], 0), NN)
        x_ref[here, :] = ek

        @pl.when(k + 1 < blocks)
        def _():
            pan = stacked(six_left(s_ref[:, here]), six_right(inv, 1), NT)
            left_ref[...] = six_left(pan)
            right_ref[...] = six_right(pan, 1)
            e_ref[...] = six_right(ek, 0)

        def under(i, inner):
            rows = pl.ds(pl.multiple_of(i * BLK, BLK), BLK)
            part = left_ref[rows, :]
            s_ref[rows, :] = s_ref[rows, :] - stacked(part, right_ref[...], NT)
            x_ref[rows, :] = x_ref[rows, :] - stacked(part, e_ref[...], NN)
            return inner

        lax.fori_loop(k + 1, blocks, under, 0)
        return carry

    lax.fori_loop(first, first + count, step, 0)


def set_identity(x_ref):
    rows = lax.broadcasted_iota(jnp.int32, x_ref.shape, 0)
    lanes = lax.broadcasted_iota(jnp.int32, x_ref.shape, 1)
    x_ref[...] = (rows == lanes).astype(F32)


def joined(core, s_ref, mine, other):
    @pl.when(core == 0)
    def _():
        s_ref[:, :HALF] = mine
        s_ref[:, HALF:] = other

    @pl.when(core == 1)
    def _():
        s_ref[:, :HALF] = other
        s_ref[:, HALF:] = mine


def first_kernel(meta, mine_ref, other_ref, x_ref, s_ref, *scratch):
    joined(meta[6], s_ref, mine_ref[...], other_ref[...])
    set_identity(x_ref)
    eliminate_blocks(0, 4, s_ref, x_ref, scratch)


def second_kernel(meta, mine_ref, other_ref, x11_ref, x_ref, l21_ref, s_ref, *scratch):
    joined(meta[6], s_ref, mine_ref[0], other_ref[0])
    l21_ref[:, :HALF] = dot_nt(s_ref[:, :HALF], x11_ref[:HALF, :HALF])
    l21_ref[:, HALF:] = dot_nt(s_ref[...], x11_ref[HALF:, :])
    joined(meta[6], s_ref, mine_ref[1], other_ref[1])
    for i in range(TILE // BLK):
        here, wide = slice(i * BLK, (i + 1) * BLK), slice(0, (i + 1) * BLK)
        s_ref[here, wide] = s_ref[here, wide] - dot_nt(l21_ref[here, :], l21_ref[wide, :])
    set_identity(x_ref)
    eliminate_blocks(0, 4, s_ref, x_ref, scratch)


def stage(kernel, args, outs, scratch, with_meta):
    vmem = pl.BlockSpec(memory_space=pltpu.VMEM)
    specs = [pl.BlockSpec(memory_space=pltpu.SMEM)] if with_meta else []
    square = jax.ShapeDtypeStruct((TILE, TILE), F32)
    return pl.pallas_call(
        kernel,
        out_shape=(square,) * outs,
        in_specs=specs + [vmem] * (len(args) - len(specs)),
        out_specs=(vmem,) * outs,
        scratch_shapes=scratch
        + [pltpu.VMEM((TILE, 6 * BLK), jnp.bfloat16)] * 2
        + [pltpu.VMEM((6 * BLK, TILE), jnp.bfloat16)],
        cost_estimate=pl.CostEstimate(flops=2 * 10**10, bytes_accessed=4 * 2**20, transcendentals=0),
    )(*args)


def first_factor(meta, mine, other):
    return stage(first_kernel, (meta, mine, other), 1, [pltpu.VMEM((TILE, TILE), F32)], True)[0]


def second_all(meta, mine, other, x11):
    args = (meta, mine, other, x11)
    return stage(second_kernel, args, 2, [pltpu.VMEM((TILE, TILE), F32)], True)


def unpack_first_kernel(v_ref, tile_ref, cross_ref, *quarters):
    for q in range(4):
        piece = v_ref[pl.ds(q, TILE, stride=4), :]
        cross_ref[:, q * BLK : (q + 1) * BLK] = piece
        if q < 2:
            tile_ref[:, q * BLK : (q + 1) * BLK] = piece
            for i, quarter in enumerate(quarters):
                quarter[:, q * BLK : (q + 1) * BLK] = piece[i * BLK : (i + 1) * BLK, :]


def unpack_first(view):
    def whole(*shape):
        return pl.BlockSpec(shape, lambda i: (0, 0))

    return pl.pallas_call(
        unpack_first_kernel,
        out_shape=(
            jax.ShapeDtypeStruct((TILE, HALF), F32),
            jax.ShapeDtypeStruct((TILE, TILE), F32),
        )
        + (jax.ShapeDtypeStruct((BLK, HALF), F32),) * 4,
        grid=(1,),
        in_specs=[whole(4 * TILE, BLK)],
        out_specs=(whole(TILE, HALF), whole(TILE, TILE)) + (whole(BLK, HALF),) * 4,
        name="unpack_first",
    )(view)


def unpack_rest_kernel(v_ref, *tiles):
    for i, tile in enumerate(tiles):

        @pl.when(pl.program_id(0) == i)
        def _():
            for q in range(2):
                tile[:, q * BLK : (q + 1) * BLK] = v_ref[pl.ds(q, TILE, stride=4), :]


def unpack_rest(view):
    return pl.pallas_call(
        unpack_rest_kernel,
        out_shape=(jax.ShapeDtypeStruct((TILE, HALF), F32),) * 3,
        grid=(3,),
        in_specs=[pl.BlockSpec((4 * TILE, BLK), lambda a: (a + 1, 0))],
        out_specs=(pl.BlockSpec((TILE, HALF), lambda a: (0, 0)),) * 3,
        name="unpack_rest",
    )(view)


ROWS = 256


def apply_kernel(meta, v_ref, high_ref, low_ref, noise_ref, *refs):
    held, (out_ref, real_ref, buf, split_ref, sem) = refs[:10], refs[10:]
    step = pl.program_id(0)
    tile, plane, pos, owner = meta[step], meta[4], meta[5], meta[7]

    def copies(i):
        spots = [(m, panel) for m in range(2) for panel in range(2)]
        if i < 3:
            sources = [held[2 * i + m].at[panel] for m, panel in spots]
        else:
            sources = [held[6 + 2 * m + panel] for m, panel in spots]
        return [
            pltpu.make_async_copy(source, buf.at[i % 2, m, panel], sem.at[i % 2, m, panel])
            for source, (m, panel) in zip(sources, spots)
        ]

    @pl.when(step == 0)
    def _():
        for copy in copies(0):
            copy.start()

    for i in range(4):

        @pl.when(step == i)
        def _():
            if i < 3:
                for copy in copies(i + 1):
                    copy.start()
            for copy in copies(i):
                copy.wait()

    slot = step % 2

    def part(at, carry):
        first = pl.multiple_of(at * ROWS, ROWS)
        rows = pl.ds(first, ROWS)
        for m in range(2):
            for panel in range(2):
                for i, value in enumerate(thirds(buf[slot, m, panel, rows, :])):
                    at_lane = i * WIDTH + (2 * m + panel) * HALF
                    split_ref[:, at_lane : at_lane + HALF] = value
        row = (tile * ZS + plane) * TILE + first + lax.broadcasted_iota(jnp.int32, (ROWS, BLK), 0)
        lane = lax.broadcasted_iota(jnp.int32, (ROWS, BLK), 1)

        def written(half, acc):
            for q in range(2):
                there = pl.ds(4 * first + 2 * half + q, ROWS, stride=4)
                base = v_ref[there, :]
                if half == 0:
                    base = jnp.where(owner == 1, 0.0, base)
                col = (half * 32 + pos) * HALF + q * BLK + lane
                res = base - acc[:, q * BLK : (q + 1) * BLK]
                out_ref[there, :] = jnp.where(row >= col, res, 0.0)

        def summed(half):
            lanes = slice(half * HALF, (half + 1) * HALF)
            small = stacked(split_ref[:, :WIDTH], low_ref[:, lanes], NN)
            return small + stacked(split_ref[:, : 2 * WIDTH], high_ref[:, lanes], NN)

        written(0, summed(0))

        @pl.when(tile >= 2)
        def _():
            written(1, summed(1))

        @pl.when(tile < 2)
        def _():
            for q in range(2):
                out_ref[pl.ds(4 * first + 2 + q, ROWS, stride=4), :] = jnp.zeros((ROWS, BLK), F32)

        real = stacked(split_ref[...], noise_ref[...], NN).T
        count = real_ref.shape[1]
        real_ref[0, :, rows] = real[2 * count : 3 * count] + real[count : 2 * count] + real[:count]
        return carry

    lax.fori_loop(0, TILE // ROWS, part, 0)


def apply_all(meta, view, high, low, drawn, real, held):
    wide = pl.BlockSpec((4 * TILE, BLK), lambda i, m: (m[i], 0))

    def whole(shape):
        return pl.BlockSpec(shape, lambda i, m: (0, 0))

    return pl.pallas_call(
        apply_kernel,
        out_shape=(
            jax.ShapeDtypeStruct(view.shape, F32),
            jax.ShapeDtypeStruct((4, real, TILE), F32),
        ),
        grid_spec=pltpu.PrefetchScalarGridSpec(
            num_scalar_prefetch=1,
            grid=(4,),
            in_specs=[wide, whole(high.shape), whole(low.shape), whole(drawn.shape)]
            + [pl.BlockSpec(memory_space=pl.ANY)] * len(held),
            out_specs=(wide, pl.BlockSpec((1, real, TILE), lambda i, m: (m[i], 0, 0))),
            scratch_shapes=[
                pltpu.VMEM((2, 2, 2, TILE, HALF), F32),
                pltpu.VMEM((ROWS, 3 * WIDTH), jnp.bfloat16),
                pltpu.SemaphoreType.DMA((2, 2, 2)),
            ],
        ),
        cost_estimate=pl.CostEstimate(flops=2 * 10**10, bytes_accessed=24 * 2**20, transcendentals=0),
        name="apply_all",
    )(meta, view, high, low, drawn, *held)


def lower_times(x, value):
    return jnp.concatenate([dot_nn(x[:HALF, :HALF], value[:HALF]), dot_nn(x[HALF:, :], value)], axis=0)


def upper_times(x, value):
    return jnp.concatenate([dot_tn(x[:, :HALF], value), dot_tn(x[HALF:, HALF:], value[HALF:])], axis=0)


def weights_kernel(meta, x11, x22, l21, c0, c1, noise, high_ref, low_ref, drawn_ref):
    pos, core, owner = meta[5], meta[6], meta[7]
    y1 = lower_times(x11[...], c0[...])
    y2 = lower_times(x22[...], c1[...] - dot_nn(l21[...], y1))

    def rhs(part, at):
        ids = at + lax.broadcasted_iota(jnp.int32, (TILE, HALF), 0)
        spot = pos * HALF + lax.broadcasted_iota(jnp.int32, (TILE, HALF), 1)
        first = jnp.where(owner == 1, jnp.where(ids == spot, -1.0, 0.0), part[:, :HALF])
        return jnp.concatenate([first, part[:, HALF:], noise[:, at : at + TILE].T], axis=1)

    w2 = upper_times(x22[...], rhs(y2, TILE))
    w1 = upper_times(x11[...], rhs(y1, 0) - dot_tn(l21[...], w2))
    blank = jnp.zeros((HALF, noise.shape[0]), jnp.bfloat16)
    for panel, both in enumerate((w1, w2)):
        for half in range(2):
            at = (panel + 2 * jnp.where(core == half, 0, 1)) * HALF
            value = both[half * HALF : (half + 1) * HALF, :]
            high, low = halves(value[:, :TILE])
            drawn = jnp.concatenate([*thirds(value[:, TILE:]), blank], axis=1)
            low_ref[pl.ds(pl.multiple_of(at, HALF), HALF), :] = low
            for i in range(3):
                here = pl.ds(pl.multiple_of(i * WIDTH + at, HALF), HALF)
                drawn_ref[here, :] = drawn
                if i < 2:
                    high_ref[here, :] = high


def make_weights(meta, x11, x22, l21, c0, c1, noise):
    vmem = pl.BlockSpec(memory_space=pltpu.VMEM)
    return pl.pallas_call(
        weights_kernel,
        out_shape=(
            jax.ShapeDtypeStruct((2 * WIDTH, TILE), jnp.bfloat16),
            jax.ShapeDtypeStruct((WIDTH, TILE), jnp.bfloat16),
            jax.ShapeDtypeStruct((3 * WIDTH, 4 * noise.shape[0]), jnp.bfloat16),
        ),
        in_specs=[pl.BlockSpec(memory_space=pltpu.SMEM)] + [vmem] * 6,
        out_specs=(vmem,) * 3,
        cost_estimate=pl.CostEstimate(flops=15 * 10**9, bytes_accessed=8 * 2**20, transcendentals=0),
        name="make_weights",
    )(meta, x11, x22, l21, c0, c1, noise)


def scattered_along_x(parts):
    got = []
    for d in (1, 2, 3):
        pairs = [((pz, 0, py, c), (pz, d, py, c)) for pz in range(ZS) for py in (0, 1) for c in range(2)]
        got.append(moved(parts[d], pairs))
    return got[0] + got[1] + got[2]


def planes(routes, value):
    return moved(
        value,
        [
            ((a, px, py, c), (b, px, py, c))
            for a, b in routes
            for px in range(XS)
            for py in range(YS)
            for c in range(2)
        ],
    )


def doubled_one(hold, z):
    got = planes(((0, 6), (1, 3)), hold)
    return jnp.where((z == 6) | (z == 3), got, hold)


def doubled_two(hold, z):
    got = planes(((0, 2), (6, 4), (1, 7), (3, 5)), hold)
    return jnp.where((z == 2) | (z == 4) | (z == 7) | (z == 5), got, hold)


def exchanged(hold, z):
    got = planes([(a, a ^ 1) for a in range(ZS)], hold)
    even = z % 2 == 0
    return jnp.where(even, hold, got), jnp.where(even, got, hold)


def square_chunks(got, y):
    arrived = [got[:32]]
    for d in (1, 2, 3):
        pairs = [
            ((pz, px, py, c), (pz, px, py + d, c)) for pz in (0, 1) for px in range(XS) for py in (0, 1) for c in range(2)
        ]
        arrived.append(moved(got[32 * d : 32 * (d + 1)], pairs))

    def picked(at):
        return jnp.where(at == 0, arrived[0], jnp.where(at == 1, arrived[1], jnp.where(at == 2, arrived[2], arrived[3])))

    return jnp.stack([picked(y), picked(jnp.mod(y - 1, YS))])


def gathered_along_y(parts, firsts, y):
    ring = [parts] + [shifted(parts, dy=d) for d in (1, 2, 3)]
    return jnp.stack(
        [turned([p[m] for p in ring], jnp.mod(y - f, YS)).reshape(128, HALF) for m, f in enumerate(firsts)]
    )


def gathered_along_x(line, x):
    ring = [line] + [shifted(line, dx=d) for d in (1, 2, 3)]
    return jnp.moveaxis(turned(ring, x), 0, 1).reshape(line.shape[0], TILE, HALF)


def y_hop(routes, value):
    return moved(
        value,
        [((pz, px, a, c), (pz, px, b, c)) for a, b in routes for pz in range(ZS) for px in range(XS) for c in range(2)],
    )


def shards(covariance, noise):
    z = lax.axis_index("row").astype(jnp.int32)
    pos = 31 - lax.axis_index("col").astype(jnp.int32)
    x, y, k = pos // 8, (pos // 2) % 4, pos % 2
    owner = (pos < 4).astype(jnp.int32)
    view = covariance.reshape(-1, BLK)
    tile0, cross, *quarters = unpack_first(view)
    meta = jnp.stack([x, jnp.mod(x + 3, XS), jnp.mod(x + 1, XS), jnp.mod(x + 2, XS), z, pos, k, owner])

    quarter = jnp.where(x == 0, quarters[0], scattered_along_x(quarters))
    others = after(quarter, *unpack_rest(view))
    hold = square_chunks(quarter, y)
    tile = jnp.where(x == 0, tile0, scattered_along_x([tile0, *others]))
    hold = doubled_one(hold, z)
    hold = doubled_two(hold, z)
    first, later = exchanged(hold, z)
    cross = after(first, cross)[0]
    cross = doubled_one(cross, z)
    line = gathered_along_y(first[:1], (0,), y)
    tile, later = after(line, tile, later)
    mine = gathered_along_x(line, x)[0]
    late_line = gathered_along_y(later, (0, 1), y)
    near = y_hop(((0, 1), (1, 0)), tile)
    away = y_hop(((0, 3), (1, 2)), tile)
    far_y = y_hop(((0, 2), (1, 3)), tile)
    other = shifted(mine, swap=1)
    other, late_line, cross = tied(other, late_line, cross)
    cross = doubled_two(cross, z)
    late = gathered_along_x(late_line, x)
    x11 = first_factor(meta, mine, other)
    x11, near, away, far_y, late, cross = tied(x11, near, away, far_y, late, cross)
    late_other = shifted(late, swap=1)
    pieces = jnp.stack(
        [
            jnp.where(y == 0, tile, jnp.where(y == 1, near, jnp.where(y == 3, away, far_y))),
            jnp.where(y == 1, tile, jnp.where(y == 0, near, jnp.where(y == 2, away, far_y))),
        ]
    )
    up, down = shifted(pieces, dx=1), shifted(pieces, dx=-1)
    c0, c1 = exchanged(cross, z)
    swaps = [shifted(pieces, swap=1)]
    x22, l21 = second_all(meta, late, late_other, x11)
    x22, up, down = tied(x22, up, down)
    far0, far1 = shifted(down[0], dx=-1), shifted(up[1], dx=1)
    swaps += [shifted(up, swap=1), shifted(down, swap=1)]
    high, low, drawn = make_weights(meta, x11, x22, l21, c0, c1, jnp.swapaxes(noise, 0, 1))
    high, far0, far1 = tied(high, far0, far1)
    held = [piece for pair in zip((pieces, up, down), swaps) for piece in pair]
    held += [far0, far1, shifted(far0, swap=1), shifted(far1, swap=1)]
    factored, real = apply_all(meta, view, high, low, drawn, noise.shape[1], held)
    return factored.reshape(covariance.shape), jnp.swapaxes(real, 1, 2)[:, None]


def solution(mesh):
    placed = (P(None, "row", None, None, "col", None), P(None, "col"))
    return jax.shard_map(
        shards,
        mesh=mesh,
        in_specs=placed,
        out_specs=(P(None, "row", None, None, "col", None), P(None, "row", None, "col")),
        check_vma=False,
    )
```
